32 devices in a mesh: pack: 8 (over z, y), ctx: 4 (over x, core).
Axes of the slice: x: 2, y: 2, z: 4, core: 2. Of those that a mesh axis runs over, the one named last changes fastest.
Arguments:
- signals: bfloat16 [4096, 10240], P(('pack', 'ctx')), may hold values from -36 to 36
- state_io: bfloat16 [4096, 256], P(('pack', 'ctx')), may hold values from -0.8984375 to 0.8984375
- step_raw: bfloat16 [4096, 80], P(('pack', 'ctx')), may hold values from -4 to 4
- row_target: int32 [8, 4, 16], P('pack', 'ctx'), may hold values from 0 to 127, as said below
- table_start: int32 [8, 4], P('pack', 'ctx'), may hold values 0 or 1
- log_rate: float32 [80], replicated, may hold values from -11 to -2
- step_bias: float32 [80], replicated, may hold values from -0.5 to 0.5
- skip_gain: float32 [80], replicated, may hold values from 0.5 to 1.5
- norm_gain: float32 [5120], replicated, may hold values from 0.5 to 1.5
Outputs:
- gated: bfloat16 [4096, 5120], P(('pack', 'ctx'))
The draws below stay inside these ranges and needn't reach their ends.
Inputs may be any that keep to these rules, and one draw needn't show every extreme that they name: With t = row_target[p, c, j], t // 16 is the sequence that takes the row and t % 16 its row slot in slab c of that sequence; every slot of every slab is taken exactly once, and the rows of one device go exactly 2 to each sequence.
All inputs are finite; a program needn't handle non-finite values. No bound on the sum of `table_start` on one device may be relied on, other than what follows from the above.
Results may differ from the reference program's by a relative error of at most 0.0046.
Values may be sent and summed in bfloat16 or wider, within the bound.
A program may use at most 192 MiB of HBM per device.

```python
import math
from functools import partial
import jax
import jax.numpy as jnp
from jax import lax

HEADS = 80
HEAD_DIM = 64
STATE = 128
GROUP = 128
ROW = 8
CAP = 2
ROWS_DEV = 16
DI = 5120
SEQS = 8
SLABS = 4
SEQ_LEN = 512
GROUPS = 4
TOKENS = 4096


def draw_signals(key, part):
    key_cols, key_rows, key_vals = jax.random.split(key, 3)
    col_scale = jnp.exp(jax.random.uniform(key_cols, (2 * DI,), jnp.float32, math.log(0.3), math.log(3.0)))
    row_scale = jnp.exp(jax.random.uniform(key_rows, (TOKENS, 1), jnp.float32, math.log(0.3), math.log(3.0)))
    base_values = jnp.clip(jax.random.normal(key_vals, (TOKENS, 2 * DI), jnp.float32), -4.0, 4.0)
    return (base_values * col_scale[None, :] * row_scale).astype(jnp.bfloat16)


def draw_step_raw(key, part):
    key_offset, key_noise = jax.random.split(key, 2)
    offsets = jax.random.uniform(key_offset, (TOKENS // ROW, 1, 1), jnp.float32, -1.5, 1.0)
    noise_values = jnp.clip(0.6 * jax.random.normal(key_noise, (TOKENS // ROW, ROW, HEADS), jnp.float32), -2.4, 2.4)
    return (offsets + noise_values).reshape(TOKENS, HEADS).astype(jnp.bfloat16)


def draw_log_rate(key, part):
    key_pick, key_slow, key_fast = jax.random.split(key, 3)
    fast_share = 0.5
    fast_pick = jax.random.uniform(key_pick, (HEADS,), jnp.float32) < fast_share
    slow_log = jax.random.uniform(key_slow, (HEADS,), jnp.float32, math.log(0.1), 0.0) - jnp.log(jnp.float32(SEQ_LEN))
    fast_log = jax.random.uniform(key_fast, (HEADS,), jnp.float32, math.log(1.0 / 40.0), math.log(1.0 / 15.0))
    return jnp.where(fast_pick, fast_log, slow_log)


def seq_permutation(base_key, seq_index, length):
    return jax.random.permutation(jax.random.fold_in(base_key, seq_index), length)


def one_column(column_key):
    key_slot, key_shuffle = jax.random.split(column_key, 2)
    seq_ids = jnp.arange(SEQS, dtype=jnp.int32)
    slot_order = jax.vmap(partial(seq_permutation, key_slot, length=ROWS_DEV))(seq_ids)
    row_index = jnp.arange(ROWS_DEV, dtype=jnp.int32)
    destination = row_index // CAP
    within = row_index % CAP
    source_pos = seq_ids[:, None] * CAP + within[None, :]
    slot_taken = slot_order[destination[None, :], source_pos]
    target_value = destination[None, :] * ROWS_DEV + slot_taken
    shuffle = jax.vmap(partial(seq_permutation, key_shuffle, length=ROWS_DEV))(seq_ids)
    return jnp.take_along_axis(target_value, shuffle, axis=1)


def draw_row_target(key, part):
    column_keys = jax.vmap(partial(jax.random.fold_in, key))(jnp.arange(SLABS))
    columns = jax.vmap(one_column)(column_keys)
    return jnp.transpose(columns, (1, 0, 2)).astype(jnp.int32)


def plant(array, key, low, high):
    longest = array.shape.index(max(array.shape))
    spots = []
    for shift in (0, 1):
        where = [jax.random.randint(jax.random.fold_in(key, axis), (), 0, length) for axis, length in enumerate(array.shape)]
        where[longest] = (where[longest] + shift) % array.shape[longest]
        spots.append(tuple(where))
    return array.at[spots[0]].set(low).at[spots[1]].set(high)


def levels(stream_key, extent, cuts, low, largest):
    def one(axis_at, parts):
        steps = jax.random.uniform(jax.random.fold_in(jax.random.fold_in(stream_key, 6), axis_at), (parts,), jnp.float32, low / len(cuts), largest / len(cuts))
        return jnp.repeat(jnp.exp(steps), extent[axis_at] // parts).reshape((-1,) + (1,) * (len(extent) - axis_at - 1))

    gain = one(*cuts[0])
    for cut in cuts[1:]:
        gain = gain * one(*cut)
    return gain


def gaussian(own_key, shape, width, most, cuts=(), kind=jnp.bfloat16):
    array = width * jax.random.normal(own_key, shape, jnp.float32)
    if cuts:
        array = array * levels(own_key, shape, cuts, -0.22, 0.18)
    return jnp.clip(array, -most, most).astype(kind)


def setup_inputs(seed: int = 0) -> dict:
    splits = jax.random.split(jax.random.key(seed), 10)
    signals = draw_signals(jax.random.fold_in(splits[9], 71), 0)
    state_io = gaussian(splits[1], (TOKENS, 2 * STATE), 0.15, 0.8984375, ((0, 32),))
    step_raw = draw_step_raw(jax.random.fold_in(splits[9], 71), 0)
    row_target = draw_row_target(jax.random.fold_in(splits[9], 71), 0)
    table_start = plant((jax.random.randint(splits[4], (SEQS, GROUPS), 0, 5) < 1).astype(jnp.int32), jax.random.fold_in(splits[4], 1), 0, 1)
    log_rate = draw_log_rate(jax.random.fold_in(splits[9], 71), 0)
    step_bias = jnp.clip(jax.random.uniform(splits[6], (HEADS,), jnp.float32, -0.5, 0.5), -0.5, 0.5)
    skip_gain = jnp.clip(jax.random.uniform(splits[7], (HEADS,), jnp.float32, 0.5, 1.5), 0.5, 1.5)
    norm_gain = jnp.clip(1.0 + 0.1 * jax.random.normal(splits[8], (DI,), jnp.float32), 0.5, 1.5)
    return dict(signals=signals, state_io=state_io, step_raw=step_raw, row_target=row_target, table_start=table_start, log_rate=log_rate, step_bias=step_bias, skip_gain=skip_gain, norm_gain=norm_gain)


def group_step(state, inputs, log_rate, step_bias, skip_gain, norm_gain):
    signal_rows, io_rows, raw_rows, keep_flag = inputs
    gate_in = signal_rows[:, :DI]
    signal_in = signal_rows[:, DI:].reshape(GROUP, HEADS, HEAD_DIM)
    b_proj = io_rows[:, :STATE]
    c_proj = io_rows[:, STATE:]
    step_size = jax.nn.softplus(raw_rows.astype(jnp.float32) + step_bias)
    log_decay = -jnp.exp(log_rate) * step_size
    cumulative = jnp.cumsum(log_decay, axis=0)
    state = state * keep_flag
    c_dot_b = jnp.dot(c_proj, b_proj.T, preferred_element_type=jnp.float32)
    causal = jnp.arange(GROUP)[:, None] >= jnp.arange(GROUP)[None, :]
    per_head = cumulative.T
    log_gaps = per_head[:, :, None] - per_head[:, None, :]
    decay_mask = jnp.exp(jnp.where(causal[None], log_gaps, -jnp.inf))
    scores = (c_dot_b[None] * decay_mask * step_size.T[:, None, :]).astype(jnp.bfloat16)
    y_intra = jnp.einsum('hij,jhp->ihp', scores.astype(jnp.float32), signal_in.astype(jnp.float32))
    y_state = jnp.exp(cumulative)[:, :, None] * jnp.einsum('in,hpn->ihp', c_proj.astype(jnp.float32), state, precision=lax.Precision.HIGHEST)
    mixed = y_intra + y_state + skip_gain[None, :, None] * signal_in.astype(jnp.float32)
    to_end = jnp.exp(cumulative[-1][None, :] - cumulative) * step_size
    weighted = (signal_in.astype(jnp.float32) * to_end[:, :, None]).astype(jnp.bfloat16)
    new_state = jnp.exp(cumulative[-1])[:, None, None] * state + jnp.einsum('jhp,jn->hpn', weighted.astype(jnp.float32), b_proj.astype(jnp.float32))
    gated = mixed.reshape(GROUP, DI) * jax.nn.silu(gate_in.astype(jnp.float32))
    result = (gated * lax.rsqrt(lax.optimization_barrier(jnp.mean(gated * gated, axis=-1, keepdims=True)) + 1e-05) * norm_gain).astype(jnp.bfloat16)
    return (new_state, result)

def reference(signals, state_io, step_raw, row_target, table_start, log_rate, step_bias, skip_gain, norm_gain):
    row_total = SEQS * SLABS * ROWS_DEV
    targets = row_target.reshape(row_total).astype(jnp.int32)
    slab_of = (jnp.arange(row_total, dtype=jnp.int32) // ROWS_DEV % SLABS).astype(jnp.int32)
    placed_at = (targets // ROWS_DEV * (SLABS * ROWS_DEV) + slab_of * ROWS_DEV + targets % ROWS_DEV).astype(jnp.int32)
    source_of = jnp.zeros((row_total,), jnp.int32).at[placed_at].set(jnp.arange(row_total, dtype=jnp.int32))
    source_of = source_of.reshape(SEQS, SLABS * ROWS_DEV)
    signal_blocks = signals.reshape(row_total, ROW, 2 * DI)
    io_blocks = state_io.reshape(row_total, ROW, 2 * STATE)
    raw_blocks = step_raw.reshape(row_total, ROW, HEADS)
    keep_all = (1 - table_start).astype(jnp.float32)
    step_fn = partial(group_step, log_rate=log_rate, step_bias=step_bias, skip_gain=skip_gain, norm_gain=norm_gain)

    def one_sequence(packed):
        rows_used, keep_seq = packed

        def gather_rows(blocks):
            return jnp.take(blocks, rows_used, axis=0).reshape(GROUPS, GROUP, blocks.shape[-1])
        inputs = (gather_rows(signal_blocks), gather_rows(io_blocks), gather_rows(raw_blocks), keep_seq)
        zero_state = jnp.zeros((HEADS, HEAD_DIM, STATE), jnp.float32)
        final_state, outputs = lax.scan(step_fn, zero_state, inputs)
        return outputs.reshape(SEQ_LEN, DI)
    result = lax.map(one_sequence, (source_of, keep_all))
    return result.reshape(TOKENS, DI)
```

```python
import functools

import jax
import jax.numpy as jnp
from jax import lax
from jax.experimental import pallas as pl
from jax.experimental.pallas import tpu as pltpu
from jax.sharding import PartitionSpec as P

GROUP = 128
ROW = 8
CHUNK = 512
X_CUTS = (0.2, 0.5, 0.8)
Z_CUTS = (0.4, 0.8)
GATE_PART = 2
MESH = pl.DeviceIdType.MESH


def passed_along(block, axis, distance):
    devices = range(lax.axis_size(axis))
    route = [(i - distance, i) for i in devices if i - distance in devices]
    return lax.ppermute(block, axis, route)


def body(
    signals, state_io, step_raw, row_target, table_start, log_rate, step_bias, skip_gain, norm_gain
):
    pack_size = lax.axis_size("pack")
    ctx_size = lax.axis_size("ctx")
    row_count = row_target.shape[2]
    capacity = row_count // pack_size
    slot_count = pack_size * capacity
    inner_width = signals.shape[1] // 2
    head_count = log_rate.shape[0]
    head_width = inner_width // head_count
    state_width = state_io.shape[1] // 2
    token_count = row_count * ROW
    groups = token_count // GROUP
    targets = row_target.reshape(row_count)
    destination = targets // row_count
    row_index = jnp.arange(row_count, dtype=jnp.int32)
    earlier_rows = (destination[:, None] == destination[None, :]) & (
        row_index[None, :] < row_index[:, None]
    )
    earlier_count = jnp.sum(earlier_rows.astype(jnp.int32), axis=1)
    position = destination * capacity + earlier_count
    send_match = position[None, :] == jnp.arange(slot_count, dtype=jnp.int32)[:, None]
    send_slot = jnp.sum(jnp.where(send_match, (targets % row_count)[None, :], 0), axis=1)
    send_slot = jnp.where(jnp.any(send_match, axis=1), send_slot, -1)

    def moved(match, blocks):
        onehot = match.astype(jnp.bfloat16)
        result = jnp.einsum("sr,rtw->stw", onehot, blocks, preferred_element_type=jnp.float32)
        return result.astype(jnp.bfloat16)

    def outgoing(values):
        return moved(send_match, values.reshape(row_count, ROW, values.shape[1]))

    signal_got, io_got, raw_got, slot_got = (
        lax.all_to_all(
            outgoing(signals[:, inner_width:]), "pack", split_axis=0, concat_axis=0, tiled=True
        ),
        lax.all_to_all(outgoing(state_io), "pack", split_axis=0, concat_axis=0, tiled=True),
        lax.all_to_all(outgoing(step_raw), "pack", split_axis=0, concat_axis=0, tiled=True),
        lax.all_to_all(send_slot, "pack", split_axis=0, concat_axis=0, tiled=True),
    )
    slot_match = slot_got[None, :] == row_index[:, None]

    def arrange(values):
        return moved(slot_match, values).reshape(token_count, values.shape[-1])

    signal_in = arrange(signal_got)
    io_rows = arrange(io_got)
    raw_rows = arrange(raw_got)
    inputs = signal_in.reshape(groups, GROUP, head_count, head_width)
    b_proj = io_rows[:, :state_width].reshape(groups, GROUP, state_width)
    c_proj = io_rows[:, state_width:].reshape(groups, GROUP, state_width)
    step_size = jax.nn.softplus(raw_rows.astype(jnp.float32) + step_bias).reshape(
        groups, GROUP, head_count
    )
    log_decay = -jnp.exp(log_rate) * step_size
    causal = jnp.arange(GROUP)[:, None] >= jnp.arange(GROUP)[None, :]
    cumulative = jnp.einsum(
        "ij,kjh->kih", causal.astype(jnp.float32), log_decay, precision=lax.Precision.HIGHEST
    )
    c_dot_b = jnp.einsum("kin,kjn->kij", c_proj, b_proj, preferred_element_type=jnp.float32)
    per_head = cumulative.transpose(0, 2, 1)
    log_gaps = per_head[:, :, :, None] - per_head[:, :, None, :]
    decay_mask = jnp.exp(jnp.where(causal[None, None], log_gaps, -jnp.inf))
    scores = (c_dot_b[:, None] * decay_mask * step_size.transpose(0, 2, 1)[:, :, None, :]).astype(
        jnp.bfloat16
    )
    y_intra = jnp.einsum("khij,kjhp->kihp", scores, inputs, preferred_element_type=jnp.float32)
    to_end = jnp.exp(cumulative[:, -1:, :] - cumulative) * step_size
    weighted = (inputs.astype(jnp.float32) * to_end[..., None]).astype(jnp.bfloat16)
    local_state = jnp.einsum("kjhp,kjn->khpn", weighted, b_proj, preferred_element_type=jnp.float32)
    keep_flag = (1 - table_start.reshape(groups)).astype(jnp.float32)
    group_decay = jnp.exp(cumulative[:, -1, :])
    carry_gain = []
    carry_base = []
    gain_now = keep_flag[0] * jnp.ones((head_count,), jnp.float32)
    base_now = jnp.zeros((head_count, head_width, state_width), jnp.float32)
    for group_id in range(groups):
        if group_id > 0:
            gain_now = keep_flag[group_id] * (group_decay[group_id - 1] * gain_now)
            base_now = keep_flag[group_id] * (
                group_decay[group_id - 1][:, None, None] * base_now + local_state[group_id - 1]
            )
        carry_gain.append(gain_now)
        carry_base.append(base_now)
    leave_gain = group_decay[-1] * gain_now
    leave_base = group_decay[-1][:, None, None] * base_now + local_state[-1]
    incoming = jnp.zeros((head_count, head_width, state_width), jnp.float32)
    for hop_index in range(ctx_size - 1):
        incoming = passed_along(leave_gain[:, None, None] * incoming + leave_base, "ctx", 1)
    entering = jnp.stack(carry_gain)[:, :, None, None] * incoming[None] + jnp.stack(carry_base)
    y_state = jnp.exp(cumulative)[..., None] * jnp.einsum(
        "kin,khpn->kihp", c_proj.astype(jnp.float32), entering, precision=lax.Precision.HIGHEST
    )
    mixed = y_intra + y_state + skip_gain[None, None, :, None] * inputs.astype(jnp.float32)
    mixed = mixed.reshape(token_count, inner_width)
    gate_got = lax.all_to_all(
        outgoing(signals[:, :inner_width]), "pack", split_axis=0, concat_axis=0, tiled=True
    )
    gate_in = arrange(gate_got)
    gated = mixed * jax.nn.silu(gate_in.astype(jnp.float32))
    result = gated * lax.rsqrt(jnp.mean(gated * gated, axis=-1, keepdims=True) + 1e-05) * norm_gain
    return result.astype(jnp.bfloat16)


def exact_permute(onehot, values):
    return jnp.dot(onehot, values, preferred_element_type=jnp.float32).astype(jnp.bfloat16)


def split_sum(values):
    high = values.astype(jnp.bfloat16)
    low = (values - high.astype(jnp.float32)).astype(jnp.bfloat16)
    return jnp.concatenate([high, low], axis=1)


def fused_kernel(
    pack_size,
    ctx_size,
    head_width,
    signals_hbm,
    state_io_hbm,
    step_flip_hbm,
    row_target_hbm,
    table_start_hbm,
    log_rate_hbm,
    step_bias_hbm,
    skip_gain_hbm,
    norm_gain_hbm,
    out,
    x_in,
    z_in,
    state_io,
    step_flip,
    row_target,
    table_start,
    log_rate,
    step_bias,
    skip_gain,
    norm_gain,
    send_order,
    order,
    pieces,
    spacing,
    small,
    c_sorted,
    x_stage,
    z_stage,
    x_got,
    z_got,
    heads,
    mixed,
    squares,
    held,
    lift,
    decay,
    leave,
    enter,
    load,
    x_load,
    x_send,
    x_recv,
    z_send,
    z_recv,
    s_send,
    s_recv,
    ready,
):
    tokens = GROUP
    rows = tokens // ROW
    inner = norm_gain.shape[1]
    head_count = log_rate.shape[1]
    width = state_io.shape[1]
    state = width // 2
    block = tokens // pack_size
    chunk = CHUNK
    chunks = inner // chunk
    extra = width + 256
    x_parts = parts_of(X_CUTS, chunks)
    z_parts = parts_of(Z_CUTS, chunks)
    me = lax.axis_index("pack")
    slab = lax.axis_index("ctx")
    peers = [lax.rem(me + off, pack_size) for off in range(1, pack_size)]
    loads = [
        pltpu.make_async_copy(source, kept, load.at[i])
        for i, (source, kept) in enumerate(
            (
                (row_target_hbm, row_target),
                (state_io_hbm, state_io),
                (step_flip_hbm, step_flip),
                (signals_hbm.at[:, pl.ds(0, inner)], z_in),
                (table_start_hbm, table_start),
                (log_rate_hbm, log_rate),
                (step_bias_hbm, step_bias),
                (skip_gain_hbm, skip_gain),
                (norm_gain_hbm, norm_gain),
            )
        )
    ]
    x_loads = [
        pltpu.make_async_copy(
            signals_hbm.at[:, pl.ds(inner + low * chunk, (high - low) * chunk)],
            x_in.at[:, pl.ds(low * chunk, (high - low) * chunk)],
            x_load.at[k],
        )
        for k, (low, high) in enumerate(x_parts)
    ]
    for copy in loads[:3] + x_loads + loads[3:]:
        copy.start()
    barrier = pltpu.get_barrier_semaphore()
    for peer in peers:
        pl.semaphore_signal(barrier, inc=1, device_id={"pack": peer}, device_id_type=MESH)
    for off in range(1, ctx_size):
        pl.semaphore_signal(
            barrier, inc=1, device_id={"ctx": lax.rem(slab + off, ctx_size)}, device_id_type=MESH
        )

    lane = lax.broadcasted_iota(jnp.int32, (tokens, tokens), 1)
    sub = lax.broadcasted_iota(jnp.int32, (tokens, tokens), 0)
    head = lax.broadcasted_iota(jnp.int32, (256, chunk), 0) % 128
    column = lax.broadcasted_iota(jnp.int32, (256, chunk), 1) // head_width
    spacing[...] = head - column
    loads[0].wait()
    goal_lane = jnp.zeros((1, tokens), jnp.int32)
    goal_rows = []
    slot_rows = []
    for j in range(rows):
        target = row_target[j]
        goal = target // rows
        goal_lane = jnp.where(lane[:1] // ROW == j, goal, goal_lane)
        goal_rows.append(jnp.full((ROW, tokens), goal, jnp.int32))
        slot_rows.append(jnp.full((ROW, tokens), target - goal * rows, jnp.int32))
    goal_sub = jnp.concatenate(goal_rows, axis=0)
    slot_sub = jnp.concatenate(slot_rows, axis=0)
    earlier = (goal_sub == goal_lane) & (sub // ROW < lane // ROW) & (sub % ROW == 0)
    earlier = jnp.sum(jnp.where(earlier, 1.0, 0.0), axis=0, keepdims=True).astype(jnp.int32)
    place = (goal_lane * (rows // pack_size) + earlier) * ROW + lane[:1] % ROW
    send_order[...] = jnp.where(sub == place, 1.0, 0.0).astype(jnp.bfloat16)
    for copy in loads[1:3]:
        copy.wait()
    small[:, :width] = state_io[...]
    heads[...] = jnp.zeros(heads.shape, jnp.float32)
    heads[:head_count] = step_flip[...].astype(jnp.float32)
    small[:, width : width + 128] = heads[...].T.astype(jnp.bfloat16)
    small[:, width + 128 :] = (slot_sub * ROW + sub % ROW).astype(jnp.float32).astype(jnp.bfloat16)

    def x_span(k):
        low, high = x_parts[k]
        start = 0 if k == 0 else extra + low * chunk
        return pl.ds(start, extra + high * chunk - start)

    def x_copy(peer, slot, k):
        return pltpu.make_async_remote_copy(
            src_ref=x_stage.at[peer, :, x_span(k)],
            dst_ref=x_got.at[slot, :, x_span(k)],
            send_sem=x_send.at[k, peer],
            recv_sem=x_recv.at[k, slot],
            device_id={"pack": peer},
            device_id_type=MESH,
        )

    def z_copy(peer, slot, k):
        low, high = z_parts[k]
        columns = pl.ds(low * chunk, (high - low) * chunk)
        return pltpu.make_async_remote_copy(
            src_ref=z_stage.at[peer, :, columns],
            dst_ref=z_got.at[slot, :, columns],
            send_sem=z_send.at[k, peer],
            recv_sem=z_recv.at[k, slot],
            device_id={"pack": peer},
            device_id_type=MESH,
        )

    def s_copy(c):
        return pltpu.make_async_remote_copy(
            src_ref=leave.at[c],
            dst_ref=enter.at[c],
            send_sem=s_send.at[c],
            recv_sem=s_recv.at[c],
            device_id={"ctx": lax.rem(slab + 1, ctx_size)},
            device_id_type=MESH,
        )

    def stage_x(c):
        at = pl.multiple_of(c * chunk, chunk)
        moved = exact_permute(send_order[...], x_in[:, pl.ds(at, chunk)])
        x_stage[:, :, pl.ds(extra + at, chunk)] = moved.reshape(pack_size, block, chunk)

    def stage_z(c):
        at = pl.multiple_of(c * chunk, chunk)
        moved = exact_permute(send_order[...], z_in[:, pl.ds(at, chunk)])
        z_stage[:, :, pl.ds(at, chunk)] = moved.reshape(pack_size, block, chunk)

    x_stage[:, :, :extra] = exact_permute(send_order[...], small[...]).reshape(
        pack_size, block, extra
    )
    for k, (low, high) in enumerate(x_parts):
        x_loads[k].wait()
        pl.loop(low, high)(stage_x)
        if k == 0:
            pl.semaphore_wait(barrier, pack_size + ctx_size - 2)
        for peer in peers:
            x_copy(peer, me, k).start()
    x_got[me] = x_stage[me]

    for copy in loads[3:]:
        copy.wait()
    pl.loop(0, chunks)(stage_z)
    z_got[me] = z_stage[me]
    heads[0:8] = jnp.zeros((8, 128), jnp.float32)
    heads[0:1, :head_count] = log_rate[...]
    heads[1:2, :head_count] = step_bias[...]
    heads[2:3, :head_count] = skip_gain[...]

    def received_x(k):
        for peer in peers:
            x_copy(peer, peer, k).wait_recv()

    received_x(0)
    spot = x_got[:, :, width + 128 : extra].reshape(tokens, 128).astype(jnp.float32)
    order[...] = jnp.where(spot.T == sub.astype(jnp.float32), 1.0, 0.0).astype(jnp.bfloat16)
    maps = jnp.dot(
        order[...],
        x_got[:, :, : width + 128].reshape(tokens, width + 128),
        preferred_element_type=jnp.float32,
    )
    b_map = maps[:, :state]
    c_map = maps[:, state:width].astype(jnp.bfloat16)
    past = lane <= sub
    u = maps[:, width:] + heads[1:2, :]
    dt = jnp.maximum(u, 0.0) + jnp.log(1.0 + jnp.exp(-jnp.abs(u)))
    a = -jnp.exp(heads[0:1, :]) * dt
    cum = jnp.dot(
        jnp.where(past, 1.0, 0.0),
        a,
        preferred_element_type=jnp.float32,
        precision=lax.Precision.HIGHEST,
    )
    last = jnp.sum(a, axis=0, keepdims=True)
    mid = 0.5 * last
    dots = lax.dot_general(
        c_map,
        b_map.astype(jnp.bfloat16),
        (((1,), (1,)), ((), ())),
        preferred_element_type=jnp.float32,
    )
    c_sorted[0] = c_map
    c_sorted[1] = jnp.where(past, dots, 0.0).astype(jnp.bfloat16)
    c_sorted[2] = b_map.T.astype(jnp.bfloat16)
    keep = (1 - table_start[0, 0]).astype(jnp.float32)
    half = jnp.exp(mid)
    vectors = split_sum(
        jnp.concatenate(
            [
                half,
                keep * half,
                keep * (half * half),
                heads[2:3, :],
                jnp.zeros((4, 128), jnp.float32),
            ],
            axis=0,
        )
    )
    pieces[0:tokens] = split_sum(jnp.exp(mid - cum) * dt)
    pieces[tokens : 2 * tokens] = split_sum(jnp.exp(cum - mid))
    pieces[2 * tokens : 2 * tokens + 8] = vectors
    pieces[2 * tokens + 8 :] = jnp.zeros((8, 256), jnp.bfloat16)

    def own_slab(c):
        at = pl.multiple_of(c * chunk, chunk)
        pick = jnp.where(spacing[...] == c * (chunk // head_width), 1.0, 0.0)
        wide = jnp.dot(
            pieces[...], pick.astype(jnp.bfloat16), preferred_element_type=jnp.float32
        )
        ups = wide[tokens : 2 * tokens]
        x = jnp.dot(
            order[...],
            x_got[:, :, pl.ds(extra + at, chunk)].reshape(tokens, chunk),
            preferred_element_type=jnp.float32,
        )
        scaled = (x * wide[:tokens]).astype(jnp.bfloat16)
        leaving = wide[2 * tokens : 2 * tokens + 1] * jnp.dot(
            c_sorted[2], scaled, preferred_element_type=jnp.float32
        )

        @pl.when(slab == 0)
        def _():
            leave[c] = leaving.astype(jnp.bfloat16)
            s_copy(c).start()

        @pl.when(slab > 0)
        def _():
            held[c] = leaving
            lift[c] = ups * wide[2 * tokens + 1 : 2 * tokens + 2]
            decay[c] = wide[2 * tokens : 2 * tokens + 8]

        y = jnp.dot(c_sorted[1], scaled, preferred_element_type=jnp.float32) * ups
        mixed[:, pl.ds(at, chunk)] = y + wide[2 * tokens + 3 : 2 * tokens + 4] * x

    def earlier_slabs(low, high):
        @pl.when(slab > 0)
        def _():
            @pl.loop(low, high)
            def _(c):
                at = pl.multiple_of(c * chunk, chunk)
                s_copy(c).wait_recv()

                @pl.when(slab < ctx_size - 1)
                def _():
                    passed = decay[c, 2:3] * enter[c].astype(jnp.float32) + held[c]
                    leave[c] = passed.astype(jnp.bfloat16)
                    s_copy(c).start()

                carried = jnp.dot(c_sorted[0], enter[c], preferred_element_type=jnp.float32)
                mixed[:, pl.ds(at, chunk)] += carried * lift[c]

    for k, (low, high) in enumerate(x_parts):
        if k > 0:
            received_x(k)
        if k == GATE_PART:
            for peer in peers:
                pl.semaphore_signal(ready, inc=1, device_id={"pack": peer}, device_id_type=MESH)
        pl.loop(low, high)(own_slab)
        if k == GATE_PART:
            pl.semaphore_wait(ready, pack_size - 1)
            for part in range(len(z_parts)):
                for peer in peers:
                    z_copy(peer, me, part).start()
        if k > 0:
            earlier_slabs(*x_parts[k - 1])
    earlier_slabs(*x_parts[-1])

    squares[...] = jnp.zeros(squares.shape, jnp.float32)

    def gate(c):
        at = pl.multiple_of(c * chunk, chunk)
        z = jnp.dot(
            order[...],
            z_got[:, :, pl.ds(at, chunk)].reshape(tokens, chunk),
            preferred_element_type=jnp.float32,
        )
        g = mixed[:, pl.ds(at, chunk)] * (z / (1.0 + jnp.exp(-z)))
        mixed[:, pl.ds(at, chunk)] = g
        g = g * g
        total = g[:, :128]
        for k in range(1, chunk // 128):
            total += g[:, k * 128 : (k + 1) * 128]
        squares[...] += total

    for k, (low, high) in enumerate(z_parts):
        for peer in peers:
            z_copy(peer, peer, k).wait_recv()
        pl.loop(low, high)(gate)

    mean = jnp.sum(squares[...], axis=1, keepdims=True) * (1.0 / inner)
    squares[...] = jnp.broadcast_to(lax.rsqrt(mean + 1e-05), squares.shape)

    @pl.loop(0, chunks)
    def _(c):
        at = pl.multiple_of(c * chunk, chunk)
        scale = jnp.concatenate([squares[...]] * (chunk // 128), axis=1)
        normed = mixed[:, pl.ds(at, chunk)] * scale * norm_gain[:, pl.ds(at, chunk)]
        out[:, pl.ds(at, chunk)] = normed.astype(jnp.bfloat16)

    for peer in peers:
        for k in range(len(x_parts)):
            x_copy(peer, me, k).wait_send()
        for k in range(len(z_parts)):
            z_copy(peer, me, k).wait_send()

    @pl.when(slab < ctx_size - 1)
    def _():
        @pl.loop(0, chunks)
        def _(c):
            s_copy(c).wait_send()


def parts_of(cuts, chunks):
    ends = [max(1, round(cut * chunks)) for cut in cuts] + [chunks]
    return list(zip([0] + ends[:-1], ends))


def fused_body(
    signals, state_io, step_raw, row_target, table_start, log_rate, step_bias, skip_gain, norm_gain
):
    pack_size = lax.axis_size("pack")
    ctx_size = lax.axis_size("ctx")
    tokens = signals.shape[0]
    inner = signals.shape[1] // 2
    width = state_io.shape[1]
    state = width // 2
    head_count = log_rate.shape[0]
    block = tokens // pack_size
    chunks = inner // CHUNK
    extra = width + 256
    x_count = len(X_CUTS) + 1
    z_count = len(Z_CUTS) + 1
    hbm = pl.BlockSpec(memory_space=pltpu.HBM)
    return pl.pallas_call(
        functools.partial(fused_kernel, pack_size, ctx_size, inner // head_count),
        out_shape=jax.ShapeDtypeStruct((tokens, inner), jnp.bfloat16),
        in_specs=[hbm] * 9,
        out_specs=pl.BlockSpec(memory_space=pltpu.VMEM),
        scratch_shapes=[
            pltpu.VMEM((tokens, inner), jnp.bfloat16),
            pltpu.VMEM((tokens, inner), jnp.bfloat16),
            pltpu.VMEM((tokens, width), jnp.bfloat16),
            pltpu.VMEM((head_count, tokens), jnp.bfloat16),
            pltpu.SMEM((tokens // ROW,), jnp.int32),
            pltpu.SMEM((1, 1), jnp.int32),
            pltpu.VMEM((1, head_count), jnp.float32),
            pltpu.VMEM((1, head_count), jnp.float32),
            pltpu.VMEM((1, head_count), jnp.float32),
            pltpu.VMEM((1, inner), jnp.float32),
            pltpu.VMEM((tokens, tokens), jnp.bfloat16),
            pltpu.VMEM((tokens, tokens), jnp.bfloat16),
            pltpu.VMEM((2 * tokens + 16, 256), jnp.bfloat16),
            pltpu.VMEM((256, CHUNK), jnp.int32),
            pltpu.VMEM((tokens, extra), jnp.bfloat16),
            pltpu.VMEM((3, tokens, state), jnp.bfloat16),
            pltpu.VMEM((pack_size, block, extra + inner), jnp.bfloat16),
            pltpu.VMEM((pack_size, block, inner), jnp.bfloat16),
            pltpu.VMEM((pack_size, block, extra + inner), jnp.bfloat16),
            pltpu.VMEM((pack_size, block, inner), jnp.bfloat16),
            pltpu.VMEM((128, tokens), jnp.float32),
            pltpu.VMEM((tokens, inner), jnp.float32),
            pltpu.VMEM((tokens, 128), jnp.float32),
            pltpu.VMEM((chunks, state, CHUNK), jnp.float32),
            pltpu.VMEM((chunks, tokens, CHUNK), jnp.float32),
            pltpu.VMEM((chunks, 8, CHUNK), jnp.float32),
            pltpu.VMEM((chunks, state, CHUNK), jnp.bfloat16),
            pltpu.VMEM((chunks, state, CHUNK), jnp.bfloat16),
            pltpu.SemaphoreType.DMA((9,)),
            pltpu.SemaphoreType.DMA((x_count,)),
            pltpu.SemaphoreType.DMA((x_count, pack_size)),
            pltpu.SemaphoreType.DMA((x_count, pack_size)),
            pltpu.SemaphoreType.DMA((z_count, pack_size)),
            pltpu.SemaphoreType.DMA((z_count, pack_size)),
            pltpu.SemaphoreType.DMA((chunks,)),
            pltpu.SemaphoreType.DMA((chunks,)),
            pltpu.SemaphoreType.REGULAR,
        ],
        compiler_params=pltpu.CompilerParams(
            collective_id=0, has_side_effects=True, vmem_limit_bytes=60 * 1024 * 1024
        ),
    )(
        signals,
        state_io,
        step_raw.T,
        row_target.reshape(-1),
        table_start,
        log_rate.reshape(1, -1),
        step_bias.reshape(1, -1),
        skip_gain.reshape(1, -1),
        norm_gain.reshape(1, -1),
    )


def either_body(*arguments):
    one_group = arguments[0].shape[0] == GROUP and arguments[0].shape[1] % (2 * CHUNK) == 0
    return (fused_body if one_group else body)(*arguments)


def solution(mesh):
    return jax.shard_map(
        either_body,
        mesh=mesh,
        in_specs=(
            P(("pack", "ctx"), None),
            P(("pack", "ctx"), None),
            P(("pack", "ctx"), None),
            P("pack", "ctx", None),
            P("pack", "ctx"),
            P(),
            P(),
            P(),
            P(),
        ),
        out_specs=P(("pack", "ctx"), None),
        check_vma=False,
    )
```

```python
import functools

import jax
import jax.numpy as jnp
from jax import lax
from jax.experimental import pallas as pl
from jax.experimental.pallas import tpu as pltpu
from jax.sharding import PartitionSpec as P

GROUP = 128
ROW = 8
CHUNK = 512
X_CUTS = (0.2, 0.5, 0.8)
Z_CUTS = (0.4, 0.8)
GATE_PART = 1
MESH = pl.DeviceIdType.MESH


def passed_along(block, axis, distance):
    devices = range(lax.axis_size(axis))
    route = [(i - distance, i) for i in devices if i - distance in devices]
    return lax.ppermute(block, axis, route)


def body(
    signals, state_io, step_raw, row_target, table_start, log_rate, step_bias, skip_gain, norm_gain
):
    pack_size = lax.axis_size("pack")
    ctx_size = lax.axis_size("ctx")
    row_count = row_target.shape[2]
    capacity = row_count // pack_size
    slot_count = pack_size * capacity
    inner_width = signals.shape[1] // 2
    head_count = log_rate.shape[0]
    head_width = inner_width // head_count
    state_width = state_io.shape[1] // 2
    token_count = row_count * ROW
    groups = token_count // GROUP
    targets = row_target.reshape(row_count)
    destination = targets // row_count
    row_index = jnp.arange(row_count, dtype=jnp.int32)
    earlier_rows = (destination[:, None] == destination[None, :]) & (
        row_index[None, :] < row_index[:, None]
    )
    earlier_count = jnp.sum(earlier_rows.astype(jnp.int32), axis=1)
    position = destination * capacity + earlier_count
    send_match = position[None, :] == jnp.arange(slot_count, dtype=jnp.int32)[:, None]
    send_slot = jnp.sum(jnp.where(send_match, (targets % row_count)[None, :], 0), axis=1)
    send_slot = jnp.where(jnp.any(send_match, axis=1), send_slot, -1)

    def moved(match, blocks):
        onehot = match.astype(jnp.bfloat16)
        result = jnp.einsum("sr,rtw->stw", onehot, blocks, preferred_element_type=jnp.float32)
        return result.astype(jnp.bfloat16)

    def outgoing(values):
        return moved(send_match, values.reshape(row_count, ROW, values.shape[1]))

    signal_got, io_got, raw_got, slot_got = (
        lax.all_to_all(
            outgoing(signals[:, inner_width:]), "pack", split_axis=0, concat_axis=0, tiled=True
        ),
        lax.all_to_all(outgoing(state_io), "pack", split_axis=0, concat_axis=0, tiled=True),
        lax.all_to_all(outgoing(step_raw), "pack", split_axis=0, concat_axis=0, tiled=True),
        lax.all_to_all(send_slot, "pack", split_axis=0, concat_axis=0, tiled=True),
    )
    slot_match = slot_got[None, :] == row_index[:, None]

    def arrange(values):
        return moved(slot_match, values).reshape(token_count, values.shape[-1])

    signal_in = arrange(signal_got)
    io_rows = arrange(io_got)
    raw_rows = arrange(raw_got)
    inputs = signal_in.reshape(groups, GROUP, head_count, head_width)
    b_proj = io_rows[:, :state_width].reshape(groups, GROUP, state_width)
    c_proj = io_rows[:, state_width:].reshape(groups, GROUP, state_width)
    step_size = jax.nn.softplus(raw_rows.astype(jnp.float32) + step_bias).reshape(
        groups, GROUP, head_count
    )
    log_decay = -jnp.exp(log_rate) * step_size
    causal = jnp.arange(GROUP)[:, None] >= jnp.arange(GROUP)[None, :]
    cumulative = jnp.einsum(
        "ij,kjh->kih", causal.astype(jnp.float32), log_decay, precision=lax.Precision.HIGHEST
    )
    c_dot_b = jnp.einsum("kin,kjn->kij", c_proj, b_proj, preferred_element_type=jnp.float32)
    per_head = cumulative.transpose(0, 2, 1)
    log_gaps = per_head[:, :, :, None] - per_head[:, :, None, :]
    decay_mask = jnp.exp(jnp.where(causal[None, None], log_gaps, -jnp.inf))
    scores = (c_dot_b[:, None] * decay_mask * step_size.transpose(0, 2, 1)[:, :, None, :]).astype(
        jnp.bfloat16
    )
    y_intra = jnp.einsum("khij,kjhp->kihp", scores, inputs, preferred_element_type=jnp.float32)
    to_end = jnp.exp(cumulative[:, -1:, :] - cumulative) * step_size
    weighted = (inputs.astype(jnp.float32) * to_end[..., None]).astype(jnp.bfloat16)
    local_state = jnp.einsum("kjhp,kjn->khpn", weighted, b_proj, preferred_element_type=jnp.float32)
    keep_flag = (1 - table_start.reshape(groups)).astype(jnp.float32)
    group_decay = jnp.exp(cumulative[:, -1, :])
    carry_gain = []
    carry_base = []
    gain_now = keep_flag[0] * jnp.ones((head_count,), jnp.float32)
    base_now = jnp.zeros((head_count, head_width, state_width), jnp.float32)
    for group_id in range(groups):
        if group_id > 0:
            gain_now = keep_flag[group_id] * (group_decay[group_id - 1] * gain_now)
            base_now = keep_flag[group_id] * (
                group_decay[group_id - 1][:, None, None] * base_now + local_state[group_id - 1]
            )
        carry_gain.append(gain_now)
        carry_base.append(base_now)
    leave_gain = group_decay[-1] * gain_now
    leave_base = group_decay[-1][:, None, None] * base_now + local_state[-1]
    incoming = jnp.zeros((head_count, head_width, state_width), jnp.float32)
    for hop_index in range(ctx_size - 1):
        incoming = passed_along(leave_gain[:, None, None] * incoming + leave_base, "ctx", 1)
    entering = jnp.stack(carry_gain)[:, :, None, None] * incoming[None] + jnp.stack(carry_base)
    y_state = jnp.exp(cumulative)[..., None] * jnp.einsum(
        "kin,khpn->kihp", c_proj.astype(jnp.float32), entering, precision=lax.Precision.HIGHEST
    )
    mixed = y_intra + y_state + skip_gain[None, None, :, None] * inputs.astype(jnp.float32)
    mixed = mixed.reshape(token_count, inner_width)
    gate_got = lax.all_to_all(
        outgoing(signals[:, :inner_width]), "pack", split_axis=0, concat_axis=0, tiled=True
    )
    gate_in = arrange(gate_got)
    gated = mixed * jax.nn.silu(gate_in.astype(jnp.float32))
    result = gated * lax.rsqrt(jnp.mean(gated * gated, axis=-1, keepdims=True) + 1e-05) * norm_gain
    return result.astype(jnp.bfloat16)


def exact_permute(onehot, values):
    return jnp.dot(onehot, values, preferred_element_type=jnp.float32).astype(jnp.bfloat16)


def split_sum(values):
    high = values.astype(jnp.bfloat16)
    low = (values - high.astype(jnp.float32)).astype(jnp.bfloat16)
    return jnp.concatenate([high, low], axis=1)


def fused_kernel(
    pack_size,
    ctx_size,
    head_width,
    signals_hbm,
    state_io_hbm,
    step_flip_hbm,
    row_target_hbm,
    table_start_hbm,
    log_rate_hbm,
    step_bias_hbm,
    skip_gain_hbm,
    norm_gain_hbm,
    out,
    x_in,
    z_in,
    state_io,
    step_flip,
    row_target,
    table_start,
    log_rate,
    step_bias,
    skip_gain,
    norm_gain,
    send_order,
    order,
    pieces,
    spacing,
    small,
    c_sorted,
    x_stage,
    z_stage,
    x_got,
    z_got,
    heads,
    mixed,
    squares,
    held,
    lift,
    decay,
    leave,
    enter,
    load,
    x_load,
    x_send,
    x_recv,
    z_send,
    z_recv,
    s_send,
    s_recv,
    ready,
):
    tokens = GROUP
    rows = tokens // ROW
    inner = norm_gain.shape[1]
    head_count = log_rate.shape[1]
    width = state_io.shape[1]
    state = width // 2
    block = tokens // pack_size
    chunk = CHUNK
    chunks = inner // chunk
    extra = width + 128
    x_parts = parts_of(X_CUTS, chunks)
    z_parts = parts_of(Z_CUTS, chunks)
    me = lax.axis_index("pack")
    slab = lax.axis_index("ctx")
    peers = [lax.rem(me + off, pack_size) for off in range(1, pack_size)]
    loads = [
        pltpu.make_async_copy(source, kept, load.at[i])
        for i, (source, kept) in enumerate(
            (
                (row_target_hbm, row_target),
                (state_io_hbm, state_io),
                (step_flip_hbm, step_flip),
                (signals_hbm.at[:, pl.ds(0, inner)], z_in),
                (table_start_hbm, table_start),
                (log_rate_hbm, log_rate),
                (step_bias_hbm, step_bias),
                (skip_gain_hbm, skip_gain),
                (norm_gain_hbm, norm_gain),
            )
        )
    ]
    x_loads = [
        pltpu.make_async_copy(
            signals_hbm.at[:, pl.ds(inner + low * chunk, (high - low) * chunk)],
            x_in.at[:, pl.ds(low * chunk, (high - low) * chunk)],
            x_load.at[k],
        )
        for k, (low, high) in enumerate(x_parts)
    ]
    for copy in loads[:3] + x_loads + loads[3:]:
        copy.start()
    barrier = pltpu.get_barrier_semaphore()
    for peer in peers:
        pl.semaphore_signal(barrier, inc=1, device_id={"pack": peer}, device_id_type=MESH)
    for off in range(1, ctx_size):
        pl.semaphore_signal(
            barrier, inc=1, device_id={"ctx": lax.rem(slab + off, ctx_size)}, device_id_type=MESH
        )

    lane = lax.broadcasted_iota(jnp.int32, (tokens, tokens), 1)
    sub = lax.broadcasted_iota(jnp.int32, (tokens, tokens), 0)
    head = lax.broadcasted_iota(jnp.int32, (256, chunk), 0) % 128
    column = lax.broadcasted_iota(jnp.int32, (256, chunk), 1) // head_width
    spacing[...] = head - column
    loads[0].wait()
    goal_lane = jnp.zeros((1, tokens), jnp.int32)
    goal_rows = []
    slot_rows = []
    for j in range(rows):
        target = row_target[j]
        goal = target // rows
        goal_lane = jnp.where(lane[:1] // ROW == j, goal, goal_lane)
        goal_rows.append(jnp.full((ROW, tokens), goal, jnp.int32))
        slot_rows.append(jnp.full((ROW, tokens), target - goal * rows, jnp.int32))
    goal_sub = jnp.concatenate(goal_rows, axis=0)
    slot_sub = jnp.concatenate(slot_rows, axis=0)
    earlier = (goal_sub == goal_lane) & (sub // ROW < lane // ROW) & (sub % ROW == 0)
    earlier = jnp.sum(jnp.where(earlier, 1.0, 0.0), axis=0, keepdims=True).astype(jnp.int32)
    place = (goal_lane * (rows // pack_size) + earlier) * ROW + lane[:1] % ROW
    send_order[...] = jnp.where(sub == place, 1.0, 0.0).astype(jnp.bfloat16)
    for copy in loads[1:3]:
        copy.wait()
    small[:, :width] = state_io[...]
    heads[...] = jnp.zeros(heads.shape, jnp.float32)
    heads[:head_count] = step_flip[...].astype(jnp.float32)
    spot = (slot_sub * ROW + sub % ROW).astype(jnp.float32)
    small[:, width:] = jnp.where(lane < head_count, heads[...].T, spot).astype(jnp.bfloat16)

    def x_span(k):
        low, high = x_parts[k]
        start = 0 if k == 0 else extra + low * chunk
        return pl.ds(start, extra + high * chunk - start)

    def x_copy(peer, slot, k):
        return pltpu.make_async_remote_copy(
            src_ref=x_stage.at[peer, :, x_span(k)],
            dst_ref=x_got.at[slot, :, x_span(k)],
            send_sem=x_send.at[k, peer],
            recv_sem=x_recv.at[k, slot],
            device_id={"pack": peer},
            device_id_type=MESH,
        )

    def z_copy(peer, slot, k):
        low, high = z_parts[k]
        columns = pl.ds(low * chunk, (high - low) * chunk)
        return pltpu.make_async_remote_copy(
            src_ref=z_stage.at[peer, :, columns],
            dst_ref=z_got.at[slot, :, columns],
            send_sem=z_send.at[k, peer],
            recv_sem=z_recv.at[k, slot],
            device_id={"pack": peer},
            device_id_type=MESH,
        )

    def s_copy(c):
        return pltpu.make_async_remote_copy(
            src_ref=leave.at[c],
            dst_ref=enter.at[c],
            send_sem=s_send.at[c],
            recv_sem=s_recv.at[c],
            device_id={"ctx": lax.rem(slab + 1, ctx_size)},
            device_id_type=MESH,
        )

    def stage_x(c):
        at = pl.multiple_of(c * chunk, chunk)
        moved = exact_permute(send_order[...], x_in[:, pl.ds(at, chunk)])
        x_stage[:, :, pl.ds(extra + at, chunk)] = moved.reshape(pack_size, block, chunk)

    def stage_z(c):
        at = pl.multiple_of(c * chunk, chunk)
        moved = exact_permute(send_order[...], z_in[:, pl.ds(at, chunk)])
        z_stage[:, :, pl.ds(at, chunk)] = moved.reshape(pack_size, block, chunk)

    x_stage[:, :, :extra] = exact_permute(send_order[...], small[...]).reshape(
        pack_size, block, extra
    )
    for k, (low, high) in enumerate(x_parts):
        x_loads[k].wait()
        pl.loop(low, high)(stage_x)
        if k == 0:
            pl.semaphore_wait(barrier, pack_size + ctx_size - 2)
        for peer in peers:
            x_copy(peer, me, k).start()
    x_got[me] = x_stage[me]

    for copy in loads[3:]:
        copy.wait()
    pl.loop(0, chunks)(stage_z)
    z_got[me] = z_stage[me]
    heads[0:8] = jnp.zeros((8, 128), jnp.float32)
    heads[0:1, :head_count] = log_rate[...]
    heads[1:2, :head_count] = step_bias[...]
    heads[2:3, :head_count] = skip_gain[...]

    def received_x(k):
        for peer in peers:
            x_copy(peer, peer, k).wait_recv()

    received_x(0)
    heads_got = x_got[:, :, width:extra].reshape(tokens, 128).astype(jnp.float32).T
    spot_lane = heads_got[head_count : head_count + 1]
    order[...] = jnp.where(spot_lane == sub.astype(jnp.float32), 1.0, 0.0).astype(jnp.bfloat16)
    maps = jnp.dot(
        order[...],
        x_got[:, :, :extra].reshape(tokens, extra),
        preferred_element_type=jnp.float32,
    )
    b_map = maps[:, :state]
    c_map = maps[:, state:width].astype(jnp.bfloat16)
    past = lane <= sub
    u = jnp.where(lane < head_count, maps[:, width:], 0.0) + heads[1:2, :]
    dt = jnp.maximum(u, 0.0) + jnp.log(1.0 + jnp.exp(-jnp.abs(u)))
    a = -jnp.exp(heads[0:1, :]) * dt
    cum = jnp.dot(
        jnp.where(past, 1.0, 0.0),
        a,
        preferred_element_type=jnp.float32,
        precision=lax.Precision.HIGHEST,
    )
    last = jnp.sum(a, axis=0, keepdims=True)
    mid = 0.5 * last
    dots = lax.dot_general(
        c_map,
        b_map.astype(jnp.bfloat16),
        (((1,), (1,)), ((), ())),
        preferred_element_type=jnp.float32,
    )
    c_sorted[0] = c_map
    c_sorted[1] = jnp.where(past, dots, 0.0).astype(jnp.bfloat16)
    c_sorted[2] = b_map.T.astype(jnp.bfloat16)
    keep = (1 - table_start[0, 0]).astype(jnp.float32)
    half = jnp.exp(mid)
    vectors = split_sum(
        jnp.concatenate(
            [
                half,
                keep * half,
                keep * (half * half),
                heads[2:3, :],
                jnp.zeros((4, 128), jnp.float32),
            ],
            axis=0,
        )
    )
    pieces[0:tokens] = split_sum(jnp.exp(mid - cum) * dt)
    pieces[tokens : 2 * tokens] = split_sum(jnp.exp(cum - mid))
    pieces[2 * tokens : 2 * tokens + 8] = vectors
    pieces[2 * tokens + 8 :] = jnp.zeros((8, 256), jnp.bfloat16)

    def own_slab(c):
        at = pl.multiple_of(c * chunk, chunk)
        pick = jnp.where(spacing[...] == c * (chunk // head_width), 1.0, 0.0)
        wide = jnp.dot(
            pieces[...], pick.astype(jnp.bfloat16), preferred_element_type=jnp.float32
        )
        ups = wide[tokens : 2 * tokens]
        x = jnp.dot(
            order[...],
            x_got[:, :, pl.ds(extra + at, chunk)].reshape(tokens, chunk),
            preferred_element_type=jnp.float32,
        )
        scaled = (x * wide[:tokens]).astype(jnp.bfloat16)
        leaving = wide[2 * tokens : 2 * tokens + 1] * jnp.dot(
            c_sorted[2], scaled, preferred_element_type=jnp.float32
        )

        @pl.when(slab == 0)
        def _():
            leave[c] = leaving.astype(jnp.bfloat16)
            s_copy(c).start()

        @pl.when(slab > 0)
        def _():
            held[c] = leaving
            lift[c] = ups * wide[2 * tokens + 1 : 2 * tokens + 2]
            decay[c] = wide[2 * tokens : 2 * tokens + 8]

        y = jnp.dot(c_sorted[1], scaled, preferred_element_type=jnp.float32) * ups
        mixed[:, pl.ds(at, chunk)] = y + wide[2 * tokens + 3 : 2 * tokens + 4] * x

    def earlier_slabs(low, high):
        @pl.when(slab > 0)
        def _():
            @pl.loop(low, high)
            def _(c):
                at = pl.multiple_of(c * chunk, chunk)
                s_copy(c).wait_recv()

                @pl.when(slab < ctx_size - 1)
                def _():
                    passed = decay[c, 2:3] * enter[c].astype(jnp.float32) + held[c]
                    leave[c] = passed.astype(jnp.bfloat16)
                    s_copy(c).start()

                carried = jnp.dot(c_sorted[0], enter[c], preferred_element_type=jnp.float32)
                mixed[:, pl.ds(at, chunk)] += carried * lift[c]

    for k, (low, high) in enumerate(x_parts):
        if k > 0:
            received_x(k)
        if k == GATE_PART:
            for peer in peers:
                pl.semaphore_signal(ready, inc=1, device_id={"pack": peer}, device_id_type=MESH)
        pl.loop(low, high)(own_slab)
        if k == GATE_PART:
            pl.semaphore_wait(ready, pack_size - 1)
            for part in range(len(z_parts)):
                for peer in peers:
                    z_copy(peer, me, part).start()
        if k > 0:
            earlier_slabs(*x_parts[k - 1])
    earlier_slabs(*x_parts[-1])

    squares[...] = jnp.zeros(squares.shape, jnp.float32)

    def gate(c):
        at = pl.multiple_of(c * chunk, chunk)
        z = jnp.dot(
            order[...],
            z_got[:, :, pl.ds(at, chunk)].reshape(tokens, chunk),
            preferred_element_type=jnp.float32,
        )
        g = mixed[:, pl.ds(at, chunk)] * (z / (1.0 + jnp.exp(-z)))
        mixed[:, pl.ds(at, chunk)] = g
        g = g * g
        total = g[:, :128]
        for k in range(1, chunk // 128):
            total += g[:, k * 128 : (k + 1) * 128]
        squares[...] += total

    for k, (low, high) in enumerate(z_parts):
        for peer in peers:
            z_copy(peer, peer, k).wait_recv()
        pl.loop(low, high)(gate)

    mean = jnp.sum(squares[...], axis=1, keepdims=True) * (1.0 / inner)
    squares[...] = jnp.broadcast_to(lax.rsqrt(mean + 1e-05), squares.shape)

    @pl.loop(0, chunks)
    def _(c):
        at = pl.multiple_of(c * chunk, chunk)
        scale = jnp.concatenate([squares[...]] * (chunk // 128), axis=1)
        normed = mixed[:, pl.ds(at, chunk)] * scale * norm_gain[:, pl.ds(at, chunk)]
        out[:, pl.ds(at, chunk)] = normed.astype(jnp.bfloat16)

    for peer in peers:
        for k in range(len(x_parts)):
            x_copy(peer, me, k).wait_send()
        for k in range(len(z_parts)):
            z_copy(peer, me, k).wait_send()

    @pl.when(slab < ctx_size - 1)
    def _():
        @pl.loop(0, chunks)
        def _(c):
            s_copy(c).wait_send()


def parts_of(cuts, chunks):
    ends = [max(1, round(cut * chunks)) for cut in cuts] + [chunks]
    return list(zip([0] + ends[:-1], ends))


def fused_body(
    signals, state_io, step_raw, row_target, table_start, log_rate, step_bias, skip_gain, norm_gain
):
    pack_size = lax.axis_size("pack")
    ctx_size = lax.axis_size("ctx")
    tokens = signals.shape[0]
    inner = signals.shape[1] // 2
    width = state_io.shape[1]
    state = width // 2
    head_count = log_rate.shape[0]
    block = tokens // pack_size
    chunks = inner // CHUNK
    extra = width + 128
    x_count = len(X_CUTS) + 1
    z_count = len(Z_CUTS) + 1
    hbm = pl.BlockSpec(memory_space=pltpu.HBM)
    return pl.pallas_call(
        functools.partial(fused_kernel, pack_size, ctx_size, inner // head_count),
        out_shape=jax.ShapeDtypeStruct((tokens, inner), jnp.bfloat16),
        in_specs=[hbm] * 9,
        out_specs=pl.BlockSpec(memory_space=pltpu.VMEM),
        scratch_shapes=[
            pltpu.VMEM((tokens, inner), jnp.bfloat16),
            pltpu.VMEM((tokens, inner), jnp.bfloat16),
            pltpu.VMEM((tokens, width), jnp.bfloat16),
            pltpu.VMEM((head_count, tokens), jnp.bfloat16),
            pltpu.SMEM((tokens // ROW,), jnp.int32),
            pltpu.SMEM((1, 1), jnp.int32),
            pltpu.VMEM((1, head_count), jnp.float32),
            pltpu.VMEM((1, head_count), jnp.float32),
            pltpu.VMEM((1, head_count), jnp.float32),
            pltpu.VMEM((1, inner), jnp.float32),
            pltpu.VMEM((tokens, tokens), jnp.bfloat16),
            pltpu.VMEM((tokens, tokens), jnp.bfloat16),
            pltpu.VMEM((2 * tokens + 16, 256), jnp.bfloat16),
            pltpu.VMEM((256, CHUNK), jnp.int32),
            pltpu.VMEM((tokens, extra), jnp.bfloat16),
            pltpu.VMEM((3, tokens, state), jnp.bfloat16),
            pltpu.VMEM((pack_size, block, extra + inner), jnp.bfloat16),
            pltpu.VMEM((pack_size, block, inner), jnp.bfloat16),
            pltpu.VMEM((pack_size, block, extra + inner), jnp.bfloat16),
            pltpu.VMEM((pack_size, block, inner), jnp.bfloat16),
            pltpu.VMEM((128, tokens), jnp.float32),
            pltpu.VMEM((tokens, inner), jnp.float32),
            pltpu.VMEM((tokens, 128), jnp.float32),
            pltpu.VMEM((chunks, state, CHUNK), jnp.float32),
            pltpu.VMEM((chunks, tokens, CHUNK), jnp.float32),
            pltpu.VMEM((chunks, 8, CHUNK), jnp.float32),
            pltpu.VMEM((chunks, state, CHUNK), jnp.bfloat16),
            pltpu.VMEM((chunks, state, CHUNK), jnp.bfloat16),
            pltpu.SemaphoreType.DMA((9,)),
            pltpu.SemaphoreType.DMA((x_count,)),
            pltpu.SemaphoreType.DMA((x_count, pack_size)),
            pltpu.SemaphoreType.DMA((x_count, pack_size)),
            pltpu.SemaphoreType.DMA((z_count, pack_size)),
            pltpu.SemaphoreType.DMA((z_count, pack_size)),
            pltpu.SemaphoreType.DMA((chunks,)),
            pltpu.SemaphoreType.DMA((chunks,)),
            pltpu.SemaphoreType.REGULAR,
        ],
        compiler_params=pltpu.CompilerParams(
            collective_id=0, has_side_effects=True, vmem_limit_bytes=32 * 1024 * 1024
        ),
    )(*[pltpu.with_memory_space_constraint(v, pltpu.HBM) if v.size > 1 else v for v in (
        signals,
        state_io,
        step_raw.T,
        row_target.reshape(-1),
        table_start,
        log_rate.reshape(1, -1),
        step_bias.reshape(1, -1),
        skip_gain.reshape(1, -1),
        norm_gain.reshape(1, -1),
    )])


def either_body(*arguments):
    one_group = (
        arguments[0].shape[0] == GROUP
        and arguments[0].shape[1] % (2 * CHUNK) == 0
        and arguments[5].shape[0] < 128
    )
    return (fused_body if one_group else body)(*arguments)


def solution(mesh):
    return jax.shard_map(
        either_body,
        mesh=mesh,
        in_specs=(
            P(("pack", "ctx"), None),
            P(("pack", "ctx"), None),
            P(("pack", "ctx"), None),
            P("pack", "ctx", None),
            P("pack", "ctx"),
            P(),
            P(),
            P(),
            P(),
        ),
        out_specs=P(("pack", "ctx"), None),
        check_vma=False,
    )
```

```python
import functools

import jax
import jax.numpy as jnp
from jax import lax
from jax.experimental import pallas as pl
from jax.experimental.pallas import tpu as pltpu
from jax.sharding import PartitionSpec as P

GROUP = 128
ROW = 8
CHUNK = 512
X_CUTS = (0.3, 0.7)
Z_CUTS = (0.5,)
GATE_PART = 1
UNROLL = 2
MESH = pl.DeviceIdType.MESH


def passed_along(block, axis, distance):
    devices = range(lax.axis_size(axis))
    route = [(i - distance, i) for i in devices if i - distance in devices]
    return lax.ppermute(block, axis, route)


def body(
    signals, state_io, step_raw, row_target, table_start, log_rate, step_bias, skip_gain, norm_gain
):
    pack_size = lax.axis_size("pack")
    ctx_size = lax.axis_size("ctx")
    row_count = row_target.shape[2]
    capacity = row_count // pack_size
    slot_count = pack_size * capacity
    inner_width = signals.shape[1] // 2
    head_count = log_rate.shape[0]
    head_width = inner_width // head_count
    state_width = state_io.shape[1] // 2
    token_count = row_count * ROW
    groups = token_count // GROUP
    targets = row_target.reshape(row_count)
    destination = targets // row_count
    row_index = jnp.arange(row_count, dtype=jnp.int32)
    earlier_rows = (destination[:, None] == destination[None, :]) & (
        row_index[None, :] < row_index[:, None]
    )
    earlier_count = jnp.sum(earlier_rows.astype(jnp.int32), axis=1)
    position = destination * capacity + earlier_count
    send_match = position[None, :] == jnp.arange(slot_count, dtype=jnp.int32)[:, None]
    send_slot = jnp.sum(jnp.where(send_match, (targets % row_count)[None, :], 0), axis=1)
    send_slot = jnp.where(jnp.any(send_match, axis=1), send_slot, -1)

    def moved(match, blocks):
        onehot = match.astype(jnp.bfloat16)
        result = jnp.einsum("sr,rtw->stw", onehot, blocks, preferred_element_type=jnp.float32)
        return result.astype(jnp.bfloat16)

    def outgoing(values):
        return moved(send_match, values.reshape(row_count, ROW, values.shape[1]))

    signal_got, io_got, raw_got, slot_got = (
        lax.all_to_all(
            outgoing(signals[:, inner_width:]), "pack", split_axis=0, concat_axis=0, tiled=True
        ),
        lax.all_to_all(outgoing(state_io), "pack", split_axis=0, concat_axis=0, tiled=True),
        lax.all_to_all(outgoing(step_raw), "pack", split_axis=0, concat_axis=0, tiled=True),
        lax.all_to_all(send_slot, "pack", split_axis=0, concat_axis=0, tiled=True),
    )
    slot_match = slot_got[None, :] == row_index[:, None]

    def arrange(values):
        return moved(slot_match, values).reshape(token_count, values.shape[-1])

    signal_in = arrange(signal_got)
    io_rows = arrange(io_got)
    raw_rows = arrange(raw_got)
    inputs = signal_in.reshape(groups, GROUP, head_count, head_width)
    b_proj = io_rows[:, :state_width].reshape(groups, GROUP, state_width)
    c_proj = io_rows[:, state_width:].reshape(groups, GROUP, state_width)
    step_size = jax.nn.softplus(raw_rows.astype(jnp.float32) + step_bias).reshape(
        groups, GROUP, head_count
    )
    log_decay = -jnp.exp(log_rate) * step_size
    causal = jnp.arange(GROUP)[:, None] >= jnp.arange(GROUP)[None, :]
    cumulative = jnp.einsum(
        "ij,kjh->kih", causal.astype(jnp.float32), log_decay, precision=lax.Precision.HIGHEST
    )
    c_dot_b = jnp.einsum("kin,kjn->kij", c_proj, b_proj, preferred_element_type=jnp.float32)
    per_head = cumulative.transpose(0, 2, 1)
    log_gaps = per_head[:, :, :, None] - per_head[:, :, None, :]
    decay_mask = jnp.exp(jnp.where(causal[None, None], log_gaps, -jnp.inf))
    scores = (c_dot_b[:, None] * decay_mask * step_size.transpose(0, 2, 1)[:, :, None, :]).astype(
        jnp.bfloat16
    )
    y_intra = jnp.einsum("khij,kjhp->kihp", scores, inputs, preferred_element_type=jnp.float32)
    to_end = jnp.exp(cumulative[:, -1:, :] - cumulative) * step_size
    weighted = (inputs.astype(jnp.float32) * to_end[..., None]).astype(jnp.bfloat16)
    local_state = jnp.einsum("kjhp,kjn->khpn", weighted, b_proj, preferred_element_type=jnp.float32)
    keep_flag = (1 - table_start.reshape(groups)).astype(jnp.float32)
    group_decay = jnp.exp(cumulative[:, -1, :])
    carry_gain = []
    carry_base = []
    gain_now = keep_flag[0] * jnp.ones((head_count,), jnp.float32)
    base_now = jnp.zeros((head_count, head_width, state_width), jnp.float32)
    for group_id in range(groups):
        if group_id > 0:
            gain_now = keep_flag[group_id] * (group_decay[group_id - 1] * gain_now)
            base_now = keep_flag[group_id] * (
                group_decay[group_id - 1][:, None, None] * base_now + local_state[group_id - 1]
            )
        carry_gain.append(gain_now)
        carry_base.append(base_now)
    leave_gain = group_decay[-1] * gain_now
    leave_base = group_decay[-1][:, None, None] * base_now + local_state[-1]
    incoming = jnp.zeros((head_count, head_width, state_width), jnp.float32)
    for hop_index in range(ctx_size - 1):
        incoming = passed_along(leave_gain[:, None, None] * incoming + leave_base, "ctx", 1)
    entering = jnp.stack(carry_gain)[:, :, None, None] * incoming[None] + jnp.stack(carry_base)
    y_state = jnp.exp(cumulative)[..., None] * jnp.einsum(
        "kin,khpn->kihp", c_proj.astype(jnp.float32), entering, precision=lax.Precision.HIGHEST
    )
    mixed = y_intra + y_state + skip_gain[None, None, :, None] * inputs.astype(jnp.float32)
    mixed = mixed.reshape(token_count, inner_width)
    gate_got = lax.all_to_all(
        outgoing(signals[:, :inner_width]), "pack", split_axis=0, concat_axis=0, tiled=True
    )
    gate_in = arrange(gate_got)
    gated = mixed * jax.nn.silu(gate_in.astype(jnp.float32))
    result = gated * lax.rsqrt(jnp.mean(gated * gated, axis=-1, keepdims=True) + 1e-05) * norm_gain
    return result.astype(jnp.bfloat16)


def exact_permute(onehot, values):
    return jnp.dot(onehot, values, preferred_element_type=jnp.float32).astype(jnp.bfloat16)


def split_sum(values):
    high = values.astype(jnp.bfloat16)
    low = (values - high.astype(jnp.float32)).astype(jnp.bfloat16)
    return jnp.concatenate([high, low], axis=1)


def fused_kernel(
    pack_size,
    ctx_size,
    head_width,
    signals_hbm,
    state_io_hbm,
    step_flip_hbm,
    row_target_hbm,
    table_start_hbm,
    log_rate_hbm,
    step_bias_hbm,
    skip_gain_hbm,
    norm_gain_hbm,
    out,
    x_in,
    z_in,
    state_io,
    step_flip,
    row_target,
    table_start,
    log_rate,
    step_bias,
    skip_gain,
    norm_gain,
    send_order,
    order,
    pieces,
    spacing,
    small,
    c_sorted,
    x_stage,
    x_got,
    z_stage,
    z_got,
    heads,
    mixed,
    squares,
    held,
    wides,
    lift,
    leave,
    enter,
    load,
    x_load,
    x_send,
    x_recv,
    z_send,
    z_recv,
    s_send,
    s_recv,
    ready,
):
    tokens = GROUP
    rows = tokens // ROW
    inner = norm_gain.shape[1]
    head_count = log_rate.shape[1]
    width = state_io.shape[1]
    state = width // 2
    block = tokens // pack_size
    chunk = CHUNK
    chunks = inner // chunk
    extra = width + 128
    x_parts = parts_of(X_CUTS, chunks)
    z_parts = parts_of(Z_CUTS, chunks)
    me = lax.axis_index("pack")
    slab = lax.axis_index("ctx")
    peers = [lax.rem(me + off, pack_size) for off in range(1, pack_size)]
    barrier = pltpu.get_barrier_semaphore()
    for peer in peers:
        pl.semaphore_signal(barrier, inc=1, device_id={"pack": peer}, device_id_type=MESH)
    for off in range(1, ctx_size):
        pl.semaphore_signal(
            barrier, inc=1, device_id={"ctx": lax.rem(slab + off, ctx_size)}, device_id_type=MESH
        )

    loads = [
        pltpu.make_async_copy(source, kept, load.at[i])
        for i, (source, kept) in enumerate(
            (
                (row_target_hbm, row_target),
                (state_io_hbm, state_io),
                (step_flip_hbm, step_flip),
                (signals_hbm.at[:, pl.ds(0, inner)], z_in),
                (table_start_hbm, table_start),
                (log_rate_hbm, log_rate),
                (step_bias_hbm, step_bias),
                (skip_gain_hbm, skip_gain),
                (norm_gain_hbm, norm_gain),
            )
        )
    ]
    x_loads = [
        pltpu.make_async_copy(
            signals_hbm.at[:, pl.ds(inner + low * chunk, (high - low) * chunk)],
            x_in.at[:, pl.ds(low * chunk, (high - low) * chunk)],
            x_load.at[k],
        )
        for k, (low, high) in enumerate(x_parts)
    ]
    for copy in loads[:3] + x_loads + loads[3:]:
        copy.start()

    lane = lax.broadcasted_iota(jnp.int32, (tokens, tokens), 1)
    sub = lax.broadcasted_iota(jnp.int32, (tokens, tokens), 0)
    head = lax.broadcasted_iota(jnp.int32, (256, chunk), 0) % 128
    column = lax.broadcasted_iota(jnp.int32, (256, chunk), 1) // head_width
    spacing[...] = head - column
    loads[0].wait()
    goal_lane = jnp.zeros((1, tokens), jnp.int32)
    goal_rows = []
    slot_rows = []
    for j in range(rows):
        target = row_target[j]
        goal = target // rows
        goal_lane = jnp.where(lane[:1] // ROW == j, goal, goal_lane)
        goal_rows.append(jnp.full((ROW, tokens), goal, jnp.int32))
        slot_rows.append(jnp.full((ROW, tokens), target - goal * rows, jnp.int32))
    goal_sub = jnp.concatenate(goal_rows, axis=0)
    slot_sub = jnp.concatenate(slot_rows, axis=0)
    earlier = (goal_sub == goal_lane) & (sub // ROW < lane // ROW) & (sub % ROW == 0)
    earlier = jnp.sum(jnp.where(earlier, 1.0, 0.0), axis=0, keepdims=True).astype(jnp.int32)
    place = (goal_lane * (rows // pack_size) + earlier) * ROW + lane[:1] % ROW
    send_order[...] = jnp.where(sub == place, 1.0, 0.0).astype(jnp.bfloat16)
    for copy in loads[1:3]:
        copy.wait()
    small[:, :width] = state_io[...]
    heads[...] = jnp.zeros(heads.shape, jnp.float32)
    heads[:head_count] = step_flip[...].astype(jnp.float32)
    spot = (slot_sub * ROW + sub % ROW).astype(jnp.float32)
    small[:, width:] = jnp.where(lane < head_count, heads[...].T, spot).astype(jnp.bfloat16)

    def x_copy(peer, slot, k):
        return pltpu.make_async_remote_copy(
            src_ref=x_stage[k].at[peer],
            dst_ref=x_got[k].at[slot],
            send_sem=x_send.at[k, peer],
            recv_sem=x_recv.at[k, slot],
            device_id={"pack": peer},
            device_id_type=MESH,
        )

    def z_copy(peer, slot, k):
        return pltpu.make_async_remote_copy(
            src_ref=z_stage[k].at[peer],
            dst_ref=z_got[k].at[slot],
            send_sem=z_send.at[k, peer],
            recv_sem=z_recv.at[k, slot],
            device_id={"pack": peer},
            device_id_type=MESH,
        )

    def s_copy(c):
        return pltpu.make_async_remote_copy(
            src_ref=leave.at[c],
            dst_ref=enter.at[c],
            send_sem=s_send.at[c],
            recv_sem=s_recv.at[c],
            device_id={"ctx": lax.rem(slab + 1, ctx_size)},
            device_id_type=MESH,
        )

    def place(c, low, first):
        return pl.multiple_of(first + (c - low) * chunk, 128)

    def stage(source, target, low, high, first):
        @pl.loop(low, high)
        def _(c):
            at = pl.multiple_of(c * chunk, chunk)
            moved = exact_permute(send_order[...], source[:, pl.ds(at, chunk)])
            target[:, :, pl.ds(place(c, low, first), chunk)] = moved.reshape(
                pack_size, block, chunk
            )

    x_stage[0][:, :, :extra] = exact_permute(send_order[...], small[...]).reshape(
        pack_size, block, extra
    )
    for k, (low, high) in enumerate(x_parts):
        x_loads[k].wait()
        stage(x_in, x_stage[k], low, high, 0 if k else extra)
        if k == 0:
            pl.semaphore_wait(barrier, pack_size + ctx_size - 2)
        for peer in peers:
            x_copy(peer, me, k).start()
    for k in range(len(x_parts)):
        x_got[k][me] = x_stage[k][me]

    for copy in loads[3:]:
        copy.wait()
    for k, (low, high) in enumerate(z_parts):
        stage(z_in, z_stage[k], low, high, 0)
        z_got[k][me] = z_stage[k][me]
    heads[0:8] = jnp.zeros((8, 128), jnp.float32)
    heads[0:1, :head_count] = log_rate[...]
    heads[1:2, :head_count] = step_bias[...]
    heads[2:3, :head_count] = skip_gain[...]

    def received_x(k):
        for peer in peers:
            x_copy(peer, peer, k).wait_recv()

    received_x(0)
    heads_got = x_got[0][:, :, width:extra].reshape(tokens, 128).astype(jnp.float32).T
    spot_lane = heads_got[head_count : head_count + 1]
    order[...] = jnp.where(spot_lane == sub.astype(jnp.float32), 1.0, 0.0).astype(jnp.bfloat16)
    maps = jnp.dot(
        order[...],
        x_got[0][:, :, :extra].reshape(tokens, extra),
        preferred_element_type=jnp.float32,
    )
    b_map = maps[:, :state]
    c_map = maps[:, state:width].astype(jnp.bfloat16)
    past = lane <= sub
    u = jnp.where(lane < head_count, maps[:, width:], 0.0) + heads[1:2, :]
    dt = jnp.maximum(u, 0.0) + jnp.log(1.0 + jnp.exp(-jnp.abs(u)))
    a = -jnp.exp(heads[0:1, :]) * dt
    cum = jnp.dot(
        jnp.where(past, 1.0, 0.0),
        a,
        preferred_element_type=jnp.float32,
        precision=lax.Precision.HIGHEST,
    )
    last = jnp.sum(a, axis=0, keepdims=True)
    mid = 0.5 * last
    dots = lax.dot_general(
        c_map,
        b_map.astype(jnp.bfloat16),
        (((1,), (1,)), ((), ())),
        preferred_element_type=jnp.float32,
    )
    c_sorted[0] = c_map
    c_sorted[1] = jnp.where(past, dots, 0.0).astype(jnp.bfloat16)
    c_sorted[2] = b_map.T.astype(jnp.bfloat16)
    keep = (1 - table_start[0, 0]).astype(jnp.float32)
    half = jnp.exp(mid)
    vectors = split_sum(
        jnp.concatenate(
            [
                half,
                keep * half,
                keep * (half * half),
                heads[2:3, :],
                jnp.zeros((4, 128), jnp.float32),
            ],
            axis=0,
        )
    )
    pieces[0:tokens] = split_sum(jnp.exp(mid - cum) * dt)
    pieces[tokens : 2 * tokens] = split_sum(jnp.exp(cum - mid))
    pieces[2 * tokens : 2 * tokens + 8] = vectors
    pieces[2 * tokens + 8 :] = jnp.zeros((8, 256), jnp.bfloat16)

    @pl.loop(0, chunks)
    def _(c):
        pick = jnp.where(spacing[...] == c * (chunk // head_width), 1.0, 0.0)
        wide = jnp.dot(
            pieces[...], pick.astype(jnp.bfloat16), preferred_element_type=jnp.float32
        )
        wides[c] = wide
        lift[c] = wide[tokens : 2 * tokens] * wide[2 * tokens + 1 : 2 * tokens + 2]

    def own_slab(c, got, low, first):
        at = pl.multiple_of(c * chunk, chunk)
        x = jnp.dot(
            order[...],
            got[:, :, pl.ds(place(c, low, first), chunk)].reshape(tokens, chunk),
            preferred_element_type=jnp.float32,
        )
        scaled = (x * wides[c, :tokens]).astype(jnp.bfloat16)
        leaving = wides[c, 2 * tokens : 2 * tokens + 1] * jnp.dot(
            c_sorted[2], scaled, preferred_element_type=jnp.float32
        )

        @pl.when(slab == 0)
        def _():
            leave[c] = leaving.astype(jnp.bfloat16)
            s_copy(c).start()

        @pl.when(slab > 0)
        def _():
            held[c] = leaving

        y = jnp.dot(c_sorted[1], scaled, preferred_element_type=jnp.float32)
        y *= wides[c, tokens : 2 * tokens]
        mixed[:, pl.ds(at, chunk)] = y + wides[c, 2 * tokens + 3 : 2 * tokens + 4] * x

    def earlier_slabs(c):
        at = pl.multiple_of(c * chunk, chunk)
        s_copy(c).wait_recv()

        @pl.when(slab < ctx_size - 1)
        def _():
            passed = wides[c, 2 * tokens + 2 : 2 * tokens + 3] * enter[c].astype(jnp.float32)
            leave[c] = (passed + held[c]).astype(jnp.bfloat16)
            s_copy(c).start()

        carried = jnp.dot(c_sorted[0], enter[c], preferred_element_type=jnp.float32)
        mixed[:, pl.ds(at, chunk)] += carried * lift[c]

    for k, (low, high) in enumerate(x_parts):
        if k > 0:
            received_x(k)
        if k == GATE_PART:
            for peer in peers:
                pl.semaphore_signal(ready, inc=1, device_id={"pack": peer}, device_id_type=MESH)
        own = functools.partial(own_slab, got=x_got[k], low=low, first=0 if k else extra)
        pl.loop(low, high, unroll=UNROLL)(own)
        if k == GATE_PART:
            pl.semaphore_wait(ready, pack_size - 1)
            for part in range(len(z_parts)):
                for peer in peers:
                    z_copy(peer, me, part).start()
        if k > 0:

            @pl.when(slab > 0)
            def _():
                pl.loop(*x_parts[k - 1], unroll=UNROLL)(earlier_slabs)

    late = x_parts[-1][0]

    @pl.when((slab > 0) & (slab < ctx_size - 1))
    def _():
        pl.loop(late, chunks, unroll=UNROLL)(earlier_slabs)

    squares[...] = jnp.zeros(squares.shape, jnp.float32)

    def gate(c, got, low):
        at = pl.multiple_of(c * chunk, chunk)
        z = jnp.dot(
            order[...],
            got[:, :, pl.ds(place(c, low, 0), chunk)].reshape(tokens, chunk),
            preferred_element_type=jnp.float32,
        )
        half_z = 0.5 * z
        g = mixed[:, pl.ds(at, chunk)] * (half_z * jnp.tanh(half_z) + half_z)
        mixed[:, pl.ds(at, chunk)] = g
        g = g * g
        total = g[:, :128]
        for k in range(1, chunk // 128):
            total += g[:, k * 128 : (k + 1) * 128]
        squares[...] += total

    for k, (low, high) in enumerate(z_parts):
        for peer in peers:
            z_copy(peer, peer, k).wait_recv()
        gate_part = functools.partial(gate, got=z_got[k], low=low)
        if low < late:
            pl.loop(low, min(late, high), unroll=UNROLL)(gate_part)
        if high > late:

            @pl.when(slab < ctx_size - 1)
            def _():
                pl.loop(max(low, late), high, unroll=UNROLL)(gate_part)

            @pl.when(slab == ctx_size - 1)
            def _():
                @pl.loop(max(low, late), high)
                def _(c):
                    earlier_slabs(c)
                    gate_part(c)

    mean = jnp.sum(squares[...], axis=1, keepdims=True) * (1.0 / inner)
    squares[...] = jnp.broadcast_to(lax.rsqrt(mean + 1e-05), squares.shape)

    @pl.loop(0, chunks, unroll=2)
    def _(c):
        at = pl.multiple_of(c * chunk, chunk)
        scale = jnp.concatenate([squares[...]] * (chunk // 128), axis=1)
        normed = mixed[:, pl.ds(at, chunk)] * scale * norm_gain[:, pl.ds(at, chunk)]
        out[:, pl.ds(at, chunk)] = normed.astype(jnp.bfloat16)

    for peer in peers:
        for k in range(len(x_parts)):
            x_copy(peer, me, k).wait_send()
        for k in range(len(z_parts)):
            z_copy(peer, me, k).wait_send()

    @pl.when(slab < ctx_size - 1)
    def _():
        @pl.loop(0, chunks)
        def _(c):
            s_copy(c).wait_send()


def parts_of(cuts, chunks):
    ends = [max(1, round(cut * chunks)) for cut in cuts] + [chunks]
    return list(zip([0] + ends[:-1], ends))


def fused_body(
    signals, state_io, step_raw, row_target, table_start, log_rate, step_bias, skip_gain, norm_gain
):
    pack_size = lax.axis_size("pack")
    ctx_size = lax.axis_size("ctx")
    tokens = signals.shape[0]
    inner = signals.shape[1] // 2
    width = state_io.shape[1]
    state = width // 2
    head_count = log_rate.shape[0]
    block = tokens // pack_size
    chunks = inner // CHUNK
    extra = width + 128
    x_count = len(X_CUTS) + 1
    z_count = len(Z_CUTS) + 1
    hbm = pl.BlockSpec(memory_space=pltpu.HBM)
    x_buffers = [
        pltpu.VMEM((pack_size, block, (high - low) * CHUNK + (0 if k else extra)), jnp.bfloat16)
        for k, (low, high) in enumerate(parts_of(X_CUTS, chunks))
    ]
    z_buffers = [
        pltpu.VMEM((pack_size, block, (high - low) * CHUNK), jnp.bfloat16)
        for low, high in parts_of(Z_CUTS, chunks)
    ]
    return pl.pallas_call(
        functools.partial(fused_kernel, pack_size, ctx_size, inner // head_count),
        out_shape=jax.ShapeDtypeStruct((tokens, inner), jnp.bfloat16),
        in_specs=[hbm] * 9,
        out_specs=pl.BlockSpec(memory_space=pltpu.VMEM),
        scratch_shapes=[
            pltpu.VMEM((tokens, inner), jnp.bfloat16),
            pltpu.VMEM((tokens, inner), jnp.bfloat16),
            pltpu.VMEM((tokens, width), jnp.bfloat16),
            pltpu.VMEM((head_count, tokens), jnp.bfloat16),
            pltpu.SMEM((tokens // ROW,), jnp.int32),
            pltpu.SMEM((1, 1), jnp.int32),
            pltpu.VMEM((1, head_count), jnp.float32),
            pltpu.VMEM((1, head_count), jnp.float32),
            pltpu.VMEM((1, head_count), jnp.float32),
            pltpu.VMEM((1, inner), jnp.float32),
            pltpu.VMEM((tokens, tokens), jnp.bfloat16),
            pltpu.VMEM((tokens, tokens), jnp.bfloat16),
            pltpu.VMEM((2 * tokens + 16, 256), jnp.bfloat16),
            pltpu.VMEM((256, CHUNK), jnp.int32),
            pltpu.VMEM((tokens, extra), jnp.bfloat16),
            pltpu.VMEM((3, tokens, state), jnp.bfloat16),
            x_buffers,
            x_buffers,
            z_buffers,
            z_buffers,
            pltpu.VMEM((128, tokens), jnp.float32),
            pltpu.VMEM((tokens, inner), jnp.float32),
            pltpu.VMEM((tokens, 128), jnp.float32),
            pltpu.VMEM((chunks, state, CHUNK), jnp.float32),
            pltpu.VMEM((chunks, 2 * tokens + 16, CHUNK), jnp.float32),
            pltpu.VMEM((chunks, tokens, CHUNK), jnp.float32),
            pltpu.VMEM((chunks, state, CHUNK), jnp.bfloat16),
            pltpu.VMEM((chunks, state, CHUNK), jnp.bfloat16),
            pltpu.SemaphoreType.DMA((9,)),
            pltpu.SemaphoreType.DMA((x_count,)),
            pltpu.SemaphoreType.DMA((x_count, pack_size)),
            pltpu.SemaphoreType.DMA((x_count, pack_size)),
            pltpu.SemaphoreType.DMA((z_count, pack_size)),
            pltpu.SemaphoreType.DMA((z_count, pack_size)),
            pltpu.SemaphoreType.DMA((chunks,)),
            pltpu.SemaphoreType.DMA((chunks,)),
            pltpu.SemaphoreType.REGULAR,
        ],
        compiler_params=pltpu.CompilerParams(
            collective_id=0, has_side_effects=True, vmem_limit_bytes=32 * 1024 * 1024
        ),
    )(*[pltpu.with_memory_space_constraint(v, pltpu.HBM) if v.size > 1 else v for v in (
        signals,
        state_io,
        step_raw.T,
        row_target.reshape(-1),
        table_start,
        log_rate.reshape(1, -1),
        step_bias.reshape(1, -1),
        skip_gain.reshape(1, -1),
        norm_gain.reshape(1, -1),
    )])


def either_body(*arguments):
    one_group = (
        arguments[0].shape[0] == GROUP
        and arguments[0].shape[1] % (2 * CHUNK) == 0
        and arguments[5].shape[0] < 128
    )
    return (fused_body if one_group else body)(*arguments)


def solution(mesh):
    return jax.shard_map(
        either_body,
        mesh=mesh,
        in_specs=(
            P(("pack", "ctx"), None),
            P(("pack", "ctx"), None),
            P(("pack", "ctx"), None),
            P("pack", "ctx", None),
            P("pack", "ctx"),
            P(),
            P(),
            P(),
            P(),
        ),
        out_specs=P(("pack", "ctx"), None),
        check_vma=False,
    )
```

```python
import functools

import jax
import jax.numpy as jnp
from jax import lax
from jax.experimental import pallas as pl
from jax.experimental.pallas import tpu as pltpu
from jax.sharding import PartitionSpec as P

GROUP = 128
ROW = 8
CHUNK = 512
X_CUTS = (0.3, 0.7)
Z_CUTS = (0.5,)
GATE_PART = 1
UNROLL = 2
MESH = pl.DeviceIdType.MESH


def passed_along(block, axis, distance):
    devices = range(lax.axis_size(axis))
    route = [(i - distance, i) for i in devices if i - distance in devices]
    return lax.ppermute(block, axis, route)


def body(
    signals, state_io, step_raw, row_target, table_start, log_rate, step_bias, skip_gain, norm_gain
):
    pack_size = lax.axis_size("pack")
    ctx_size = lax.axis_size("ctx")
    row_count = row_target.shape[2]
    capacity = row_count // pack_size
    slot_count = pack_size * capacity
    inner_width = signals.shape[1] // 2
    head_count = log_rate.shape[0]
    head_width = inner_width // head_count
    state_width = state_io.shape[1] // 2
    token_count = row_count * ROW
    groups = token_count // GROUP
    targets = row_target.reshape(row_count)
    destination = targets // row_count
    row_index = jnp.arange(row_count, dtype=jnp.int32)
    earlier_rows = (destination[:, None] == destination[None, :]) & (
        row_index[None, :] < row_index[:, None]
    )
    earlier_count = jnp.sum(earlier_rows.astype(jnp.int32), axis=1)
    position = destination * capacity + earlier_count
    send_match = position[None, :] == jnp.arange(slot_count, dtype=jnp.int32)[:, None]
    send_slot = jnp.sum(jnp.where(send_match, (targets % row_count)[None, :], 0), axis=1)
    send_slot = jnp.where(jnp.any(send_match, axis=1), send_slot, -1)

    def moved(match, blocks):
        onehot = match.astype(jnp.bfloat16)
        result = jnp.einsum("sr,rtw->stw", onehot, blocks, preferred_element_type=jnp.float32)
        return result.astype(jnp.bfloat16)

    def outgoing(values):
        return moved(send_match, values.reshape(row_count, ROW, values.shape[1]))

    signal_got, io_got, raw_got, slot_got = (
        lax.all_to_all(
            outgoing(signals[:, inner_width:]), "pack", split_axis=0, concat_axis=0, tiled=True
        ),
        lax.all_to_all(outgoing(state_io), "pack", split_axis=0, concat_axis=0, tiled=True),
        lax.all_to_all(outgoing(step_raw), "pack", split_axis=0, concat_axis=0, tiled=True),
        lax.all_to_all(send_slot, "pack", split_axis=0, concat_axis=0, tiled=True),
    )
    slot_match = slot_got[None, :] == row_index[:, None]

    def arrange(values):
        return moved(slot_match, values).reshape(token_count, values.shape[-1])

    signal_in = arrange(signal_got)
    io_rows = arrange(io_got)
    raw_rows = arrange(raw_got)
    inputs = signal_in.reshape(groups, GROUP, head_count, head_width)
    b_proj = io_rows[:, :state_width].reshape(groups, GROUP, state_width)
    c_proj = io_rows[:, state_width:].reshape(groups, GROUP, state_width)
    step_size = jax.nn.softplus(raw_rows.astype(jnp.float32) + step_bias).reshape(
        groups, GROUP, head_count
    )
    log_decay = -jnp.exp(log_rate) * step_size
    causal = jnp.arange(GROUP)[:, None] >= jnp.arange(GROUP)[None, :]
    cumulative = jnp.einsum(
        "ij,kjh->kih", causal.astype(jnp.float32), log_decay, precision=lax.Precision.HIGHEST
    )
    c_dot_b = jnp.einsum("kin,kjn->kij", c_proj, b_proj, preferred_element_type=jnp.float32)
    per_head = cumulative.transpose(0, 2, 1)
    log_gaps = per_head[:, :, :, None] - per_head[:, :, None, :]
    decay_mask = jnp.exp(jnp.where(causal[None, None], log_gaps, -jnp.inf))
    scores = (c_dot_b[:, None] * decay_mask * step_size.transpose(0, 2, 1)[:, :, None, :]).astype(
        jnp.bfloat16
    )
    y_intra = jnp.einsum("khij,kjhp->kihp", scores, inputs, preferred_element_type=jnp.float32)
    to_end = jnp.exp(cumulative[:, -1:, :] - cumulative) * step_size
    weighted = (inputs.astype(jnp.float32) * to_end[..., None]).astype(jnp.bfloat16)
    local_state = jnp.einsum("kjhp,kjn->khpn", weighted, b_proj, preferred_element_type=jnp.float32)
    keep_flag = (1 - table_start.reshape(groups)).astype(jnp.float32)
    group_decay = jnp.exp(cumulative[:, -1, :])
    carry_gain = []
    carry_base = []
    gain_now = keep_flag[0] * jnp.ones((head_count,), jnp.float32)
    base_now = jnp.zeros((head_count, head_width, state_width), jnp.float32)
    for group_id in range(groups):
        if group_id > 0:
            gain_now = keep_flag[group_id] * (group_decay[group_id - 1] * gain_now)
            base_now = keep_flag[group_id] * (
                group_decay[group_id - 1][:, None, None] * base_now + local_state[group_id - 1]
            )
        carry_gain.append(gain_now)
        carry_base.append(base_now)
    leave_gain = group_decay[-1] * gain_now
    leave_base = group_decay[-1][:, None, None] * base_now + local_state[-1]
    incoming = jnp.zeros((head_count, head_width, state_width), jnp.float32)
    for hop_index in range(ctx_size - 1):
        incoming = passed_along(leave_gain[:, None, None] * incoming + leave_base, "ctx", 1)
    entering = jnp.stack(carry_gain)[:, :, None, None] * incoming[None] + jnp.stack(carry_base)
    y_state = jnp.exp(cumulative)[..., None] * jnp.einsum(
        "kin,khpn->kihp", c_proj.astype(jnp.float32), entering, precision=lax.Precision.HIGHEST
    )
    mixed = y_intra + y_state + skip_gain[None, None, :, None] * inputs.astype(jnp.float32)
    mixed = mixed.reshape(token_count, inner_width)
    gate_got = lax.all_to_all(
        outgoing(signals[:, :inner_width]), "pack", split_axis=0, concat_axis=0, tiled=True
    )
    gate_in = arrange(gate_got)
    gated = mixed * jax.nn.silu(gate_in.astype(jnp.float32))
    result = gated * lax.rsqrt(jnp.mean(gated * gated, axis=-1, keepdims=True) + 1e-05) * norm_gain
    return result.astype(jnp.bfloat16)


def exact_permute(onehot, values):
    return jnp.dot(onehot, values, preferred_element_type=jnp.float32).astype(jnp.bfloat16)


def split_sum(values):
    high = values.astype(jnp.bfloat16)
    low = (values - high.astype(jnp.float32)).astype(jnp.bfloat16)
    return jnp.concatenate([high, low], axis=1)


def fused_kernel(
    pack_size,
    ctx_size,
    head_width,
    signals_hbm,
    state_io_hbm,
    step_flip_hbm,
    row_target_hbm,
    table_start_hbm,
    log_rate_hbm,
    step_bias_hbm,
    skip_gain_hbm,
    norm_gain_hbm,
    out,
    x_in,
    z_in,
    state_io,
    step_flip,
    row_target,
    table_start,
    log_rate,
    step_bias,
    skip_gain,
    norm_gain,
    send_order,
    order,
    pieces,
    spacing,
    small,
    c_sorted,
    x_stage,
    x_got,
    z_stage,
    z_got,
    heads,
    mixed,
    squares,
    held,
    wides,
    lift,
    leave,
    enter,
    load,
    x_load,
    x_send,
    x_recv,
    z_send,
    z_recv,
    s_send,
    s_recv,
    ready,
):
    tokens = GROUP
    rows = tokens // ROW
    inner = norm_gain.shape[1]
    head_count = log_rate.shape[1]
    width = state_io.shape[1]
    state = width // 2
    block = tokens // pack_size
    chunk = CHUNK
    chunks = inner // chunk
    extra = width + 128
    x_parts = parts_of(X_CUTS, chunks)
    z_parts = parts_of(Z_CUTS, chunks)
    me = lax.axis_index("pack")
    slab = lax.axis_index("ctx")
    peers = [lax.rem(me + off, pack_size) for off in range(1, pack_size)]
    barrier = pltpu.get_barrier_semaphore()
    for peer in peers:
        pl.semaphore_signal(barrier, inc=1, device_id={"pack": peer}, device_id_type=MESH)
    for off in range(1, ctx_size):
        pl.semaphore_signal(
            barrier, inc=1, device_id={"ctx": lax.rem(slab + off, ctx_size)}, device_id_type=MESH
        )

    loads = [
        pltpu.make_async_copy(source, kept, load.at[i])
        for i, (source, kept) in enumerate(
            (
                (row_target_hbm, row_target),
                (state_io_hbm, state_io),
                (step_flip_hbm, step_flip),
                (signals_hbm.at[:, pl.ds(0, inner)], z_in),
                (table_start_hbm, table_start),
                (log_rate_hbm, log_rate),
                (step_bias_hbm, step_bias),
                (skip_gain_hbm, skip_gain),
                (norm_gain_hbm, norm_gain),
            )
        )
    ]
    x_loads = [
        pltpu.make_async_copy(
            signals_hbm.at[:, pl.ds(inner + low * chunk, (high - low) * chunk)],
            x_in.at[:, pl.ds(low * chunk, (high - low) * chunk)],
            x_load.at[k],
        )
        for k, (low, high) in enumerate(x_parts)
    ]
    for copy in loads[:3] + x_loads + loads[3:]:
        copy.start()

    lane = lax.broadcasted_iota(jnp.int32, (tokens, tokens), 1)
    sub = lax.broadcasted_iota(jnp.int32, (tokens, tokens), 0)
    head = lax.broadcasted_iota(jnp.int32, (256, chunk), 0) % 128
    column = lax.broadcasted_iota(jnp.int32, (256, chunk), 1) // head_width
    spacing[...] = head - column
    loads[0].wait()
    goal_lane = jnp.zeros((1, tokens), jnp.int32)
    goal_rows = []
    slot_rows = []
    for j in range(rows):
        target = row_target[j]
        goal = target // rows
        goal_lane = jnp.where(lane[:1] // ROW == j, goal, goal_lane)
        goal_rows.append(jnp.full((ROW, tokens), goal, jnp.int32))
        slot_rows.append(jnp.full((ROW, tokens), target - goal * rows, jnp.int32))
    goal_sub = jnp.concatenate(goal_rows, axis=0)
    slot_sub = jnp.concatenate(slot_rows, axis=0)
    earlier = (goal_sub == goal_lane) & (sub // ROW < lane // ROW) & (sub % ROW == 0)
    earlier = jnp.sum(jnp.where(earlier, 1.0, 0.0), axis=0, keepdims=True).astype(jnp.int32)
    place = (goal_lane * (rows // pack_size) + earlier) * ROW + lane[:1] % ROW
    send_order[...] = jnp.where(sub == place, 1.0, 0.0).astype(jnp.bfloat16)
    for copy in loads[1:3]:
        copy.wait()
    small[:, :width] = state_io[...]
    heads[...] = jnp.zeros(heads.shape, jnp.float32)
    heads[:head_count] = step_flip[...].astype(jnp.float32)
    spot = (slot_sub * ROW + sub % ROW).astype(jnp.float32)
    small[:, width:] = jnp.where(lane < head_count, heads[...].T, spot).astype(jnp.bfloat16)

    def x_copy(peer, slot, k):
        return pltpu.make_async_remote_copy(
            src_ref=x_stage[k].at[peer],
            dst_ref=x_got[k].at[slot],
            send_sem=x_send.at[k, peer],
            recv_sem=x_recv.at[k, slot],
            device_id={"pack": peer},
            device_id_type=MESH,
        )

    def z_copy(peer, slot, k):
        return pltpu.make_async_remote_copy(
            src_ref=z_stage[k].at[peer],
            dst_ref=z_got[k].at[slot],
            send_sem=z_send.at[k, peer],
            recv_sem=z_recv.at[k, slot],
            device_id={"pack": peer},
            device_id_type=MESH,
        )

    def s_copy(c):
        return pltpu.make_async_remote_copy(
            src_ref=leave.at[c],
            dst_ref=enter.at[c],
            send_sem=s_send.at[c],
            recv_sem=s_recv.at[c],
            device_id={"ctx": lax.rem(slab + 1, ctx_size)},
            device_id_type=MESH,
        )

    def place(c, low, first):
        return pl.multiple_of(first + (c - low) * chunk, 128)

    def stage(source, target, low, high, first):
        @pl.loop(low, high)
        def _(c):
            at = pl.multiple_of(c * chunk, chunk)
            moved = exact_permute(send_order[...], source[:, pl.ds(at, chunk)])
            target[:, :, pl.ds(place(c, low, first), chunk)] = moved.reshape(
                pack_size, block, chunk
            )

    x_stage[0][:, :, :extra] = exact_permute(send_order[...], small[...]).reshape(
        pack_size, block, extra
    )
    for k, (low, high) in enumerate(x_parts):
        x_loads[k].wait()
        stage(x_in, x_stage[k], low, high, 0 if k else extra)
        if k == 0:
            pl.semaphore_wait(barrier, pack_size + ctx_size - 2)
        for peer in peers:
            x_copy(peer, me, k).start()
    for k in range(len(x_parts)):
        x_got[k][me] = x_stage[k][me]

    for copy in loads[3:]:
        copy.wait()
    for k, (low, high) in enumerate(z_parts):
        stage(z_in, z_stage[k], low, high, 0)
        z_got[k][me] = z_stage[k][me]
    heads[0:8] = jnp.zeros((8, 128), jnp.float32)
    heads[0:1, :head_count] = log_rate[...]
    heads[1:2, :head_count] = step_bias[...]
    heads[2:3, :head_count] = skip_gain[...]

    def received_x(k):
        for peer in peers:
            x_copy(peer, peer, k).wait_recv()

    received_x(0)
    heads_got = x_got[0][:, :, width:extra].reshape(tokens, 128).astype(jnp.float32).T
    spot_lane = heads_got[head_count : head_count + 1]
    order[...] = jnp.where(spot_lane == sub.astype(jnp.float32), 1.0, 0.0).astype(jnp.bfloat16)
    maps = jnp.dot(
        order[...],
        x_got[0][:, :, :extra].reshape(tokens, extra),
        preferred_element_type=jnp.float32,
    )
    b_map = maps[:, :state]
    c_map = maps[:, state:width].astype(jnp.bfloat16)
    past = lane <= sub
    u = jnp.where(lane < head_count, maps[:, width:], 0.0) + heads[1:2, :]
    dt = jnp.maximum(u, 0.0) + jnp.log(1.0 + jnp.exp(-jnp.abs(u)))
    a = -jnp.exp(heads[0:1, :]) * dt
    cum = jnp.dot(
        jnp.where(past, 1.0, 0.0),
        a,
        preferred_element_type=jnp.float32,
        precision=lax.Precision.HIGHEST,
    )
    last = jnp.sum(a, axis=0, keepdims=True)
    mid = 0.5 * last
    dots = lax.dot_general(
        c_map,
        b_map.astype(jnp.bfloat16),
        (((1,), (1,)), ((), ())),
        preferred_element_type=jnp.float32,
    )
    c_sorted[0] = c_map
    c_sorted[1] = jnp.where(past, dots, 0.0).astype(jnp.bfloat16)
    c_sorted[2] = b_map.T.astype(jnp.bfloat16)
    keep = (1 - table_start[0, 0]).astype(jnp.float32)
    half = jnp.exp(mid)
    vectors = split_sum(
        jnp.concatenate(
            [
                half,
                keep * half,
                keep * (half * half),
                heads[2:3, :],
                jnp.zeros((4, 128), jnp.float32),
            ],
            axis=0,
        )
    )
    pieces[0:tokens] = split_sum(jnp.exp(mid - cum) * dt)
    pieces[tokens : 2 * tokens] = split_sum(jnp.exp(cum - mid))
    pieces[2 * tokens : 2 * tokens + 8] = vectors
    pieces[2 * tokens + 8 :] = jnp.zeros((8, 256), jnp.bfloat16)

    @pl.loop(0, chunks)
    def _(c):
        pick = jnp.where(spacing[...] == c * (chunk // head_width), 1.0, 0.0)
        wide = jnp.dot(
            pieces[...], pick.astype(jnp.bfloat16), preferred_element_type=jnp.float32
        )
        wides[c] = wide
        lift[c] = wide[tokens : 2 * tokens] * wide[2 * tokens + 1 : 2 * tokens + 2]

    def own_slab(c, got, low, first):
        at = pl.multiple_of(c * chunk, chunk)
        x = jnp.dot(
            order[...],
            got[:, :, pl.ds(place(c, low, first), chunk)].reshape(tokens, chunk),
            preferred_element_type=jnp.float32,
        )
        scaled = (x * wides[c, :tokens]).astype(jnp.bfloat16)
        leaving = wides[c, 2 * tokens : 2 * tokens + 1] * jnp.dot(
            c_sorted[2], scaled, preferred_element_type=jnp.float32
        )

        @pl.when(slab == 0)
        def _():
            leave[c] = leaving.astype(jnp.bfloat16)
            s_copy(c).start()

        @pl.when(slab > 0)
        def _():
            held[c] = leaving

        y = jnp.dot(c_sorted[1], scaled, preferred_element_type=jnp.float32)
        y *= wides[c, tokens : 2 * tokens]
        mixed[:, pl.ds(at, chunk)] = y + wides[c, 2 * tokens + 3 : 2 * tokens + 4] * x

    def earlier_slabs(c):
        at = pl.multiple_of(c * chunk, chunk)
        s_copy(c).wait_recv()

        @pl.when(slab < ctx_size - 1)
        def _():
            passed = wides[c, 2 * tokens + 2 : 2 * tokens + 3] * enter[c].astype(jnp.float32)
            leave[c] = (passed + held[c]).astype(jnp.bfloat16)
            s_copy(c).start()

        carried = jnp.dot(c_sorted[0], enter[c], preferred_element_type=jnp.float32)
        mixed[:, pl.ds(at, chunk)] += carried * lift[c]

    for k, (low, high) in enumerate(x_parts):
        if k > 0:
            received_x(k)
        if k == GATE_PART:
            for peer in peers:
                pl.semaphore_signal(ready, inc=1, device_id={"pack": peer}, device_id_type=MESH)
        own = functools.partial(own_slab, got=x_got[k], low=low, first=0 if k else extra)
        pl.loop(low, high, unroll=UNROLL)(own)
        if k == GATE_PART:
            pl.semaphore_wait(ready, pack_size - 1)
            for part in range(len(z_parts)):
                for peer in peers:
                    z_copy(peer, me, part).start()
        if k > 0:

            @pl.when(slab > 0)
            def _():
                pl.loop(*x_parts[k - 1], unroll=UNROLL)(earlier_slabs)

    late = x_parts[-1][0]

    @pl.when((slab > 0) & (slab < ctx_size - 1))
    def _():
        pl.loop(late, chunks, unroll=UNROLL)(earlier_slabs)

    squares[...] = jnp.zeros(squares.shape, jnp.float32)
    for peer in peers:
        for k in range(len(x_parts)):
            x_copy(peer, me, k).wait_send()

    @pl.when(slab < ctx_size - 1)
    def _():
        @pl.loop(0, chunks)
        def _(c):
            s_copy(c).wait_send()


    def gate(c, got, low):
        at = pl.multiple_of(c * chunk, chunk)
        z = jnp.dot(
            order[...],
            got[:, :, pl.ds(place(c, low, 0), chunk)].reshape(tokens, chunk),
            preferred_element_type=jnp.float32,
        )
        half_z = 0.5 * z
        g = mixed[:, pl.ds(at, chunk)] * (half_z * jnp.tanh(half_z) + half_z)
        mixed[:, pl.ds(at, chunk)] = g
        g = g * g
        total = g[:, :128]
        for k in range(1, chunk // 128):
            total += g[:, k * 128 : (k + 1) * 128]
        squares[...] += total

    for k, (low, high) in enumerate(z_parts):
        for peer in peers:
            z_copy(peer, peer, k).wait_recv()
        gate_part = functools.partial(gate, got=z_got[k], low=low)
        if low < late:
            pl.loop(low, min(late, high), unroll=UNROLL)(gate_part)
        if high > late:

            @pl.when(slab < ctx_size - 1)
            def _():
                pl.loop(max(low, late), high, unroll=UNROLL)(gate_part)

            @pl.when(slab == ctx_size - 1)
            def _():
                @pl.loop(max(low, late), high)
                def _(c):
                    earlier_slabs(c)
                    gate_part(c)

        if k < len(z_parts) - 1:
            for peer in peers:
                z_copy(peer, me, k).wait_send()

    mean = jnp.sum(squares[...], axis=1, keepdims=True) * (1.0 / inner)
    squares[...] = jnp.broadcast_to(lax.rsqrt(mean + 1e-05), squares.shape)

    @pl.loop(0, chunks, unroll=2)
    def _(c):
        at = pl.multiple_of(c * chunk, chunk)
        scale = jnp.concatenate([squares[...]] * (chunk // 128), axis=1)
        normed = mixed[:, pl.ds(at, chunk)] * scale * norm_gain[:, pl.ds(at, chunk)]
        out[:, pl.ds(at, chunk)] = normed.astype(jnp.bfloat16)

    for peer in peers:
        z_copy(peer, me, len(z_parts) - 1).wait_send()


def parts_of(cuts, chunks):
    ends = [max(1, round(cut * chunks)) for cut in cuts] + [chunks]
    return list(zip([0] + ends[:-1], ends))


def fused_body(
    signals, state_io, step_raw, row_target, table_start, log_rate, step_bias, skip_gain, norm_gain
):
    pack_size = lax.axis_size("pack")
    ctx_size = lax.axis_size("ctx")
    tokens = signals.shape[0]
    inner = signals.shape[1] // 2
    width = state_io.shape[1]
    state = width // 2
    head_count = log_rate.shape[0]
    block = tokens // pack_size
    chunks = inner // CHUNK
    extra = width + 128
    x_count = len(X_CUTS) + 1
    z_count = len(Z_CUTS) + 1
    hbm = pl.BlockSpec(memory_space=pltpu.HBM)
    x_buffers = [
        pltpu.VMEM((pack_size, block, (high - low) * CHUNK + (0 if k else extra)), jnp.bfloat16)
        for k, (low, high) in enumerate(parts_of(X_CUTS, chunks))
    ]
    z_buffers = [
        pltpu.VMEM((pack_size, block, (high - low) * CHUNK), jnp.bfloat16)
        for low, high in parts_of(Z_CUTS, chunks)
    ]
    return pl.pallas_call(
        functools.partial(fused_kernel, pack_size, ctx_size, inner // head_count),
        out_shape=jax.ShapeDtypeStruct((tokens, inner), jnp.bfloat16),
        in_specs=[hbm] * 9,
        out_specs=pl.BlockSpec(memory_space=pltpu.VMEM),
        scratch_shapes=[
            pltpu.VMEM((tokens, inner), jnp.bfloat16),
            pltpu.VMEM((tokens, inner), jnp.bfloat16),
            pltpu.VMEM((tokens, width), jnp.bfloat16),
            pltpu.VMEM((head_count, tokens), jnp.bfloat16),
            pltpu.SMEM((tokens // ROW,), jnp.int32),
            pltpu.SMEM((1, 1), jnp.int32),
            pltpu.VMEM((1, head_count), jnp.float32),
            pltpu.VMEM((1, head_count), jnp.float32),
            pltpu.VMEM((1, head_count), jnp.float32),
            pltpu.VMEM((1, inner), jnp.float32),
            pltpu.VMEM((tokens, tokens), jnp.bfloat16),
            pltpu.VMEM((tokens, tokens), jnp.bfloat16),
            pltpu.VMEM((2 * tokens + 16, 256), jnp.bfloat16),
            pltpu.VMEM((256, CHUNK), jnp.int32),
            pltpu.VMEM((tokens, extra), jnp.bfloat16),
            pltpu.VMEM((3, tokens, state), jnp.bfloat16),
            x_buffers,
            x_buffers,
            z_buffers,
            z_buffers,
            pltpu.VMEM((128, tokens), jnp.float32),
            pltpu.VMEM((tokens, inner), jnp.float32),
            pltpu.VMEM((tokens, 128), jnp.float32),
            pltpu.VMEM((chunks, state, CHUNK), jnp.float32),
            pltpu.VMEM((chunks, 2 * tokens + 16, CHUNK), jnp.float32),
            pltpu.VMEM((chunks, tokens, CHUNK), jnp.float32),
            pltpu.VMEM((chunks, state, CHUNK), jnp.bfloat16),
            pltpu.VMEM((chunks, state, CHUNK), jnp.bfloat16),
            pltpu.SemaphoreType.DMA((9,)),
            pltpu.SemaphoreType.DMA((x_count,)),
            pltpu.SemaphoreType.DMA((x_count, pack_size)),
            pltpu.SemaphoreType.DMA((x_count, pack_size)),
            pltpu.SemaphoreType.DMA((z_count, pack_size)),
            pltpu.SemaphoreType.DMA((z_count, pack_size)),
            pltpu.SemaphoreType.DMA((chunks,)),
            pltpu.SemaphoreType.DMA((chunks,)),
            pltpu.SemaphoreType.REGULAR,
        ],
        compiler_params=pltpu.CompilerParams(
            collective_id=0, has_side_effects=True, vmem_limit_bytes=32 * 1024 * 1024
        ),
    )(*[pltpu.with_memory_space_constraint(v, pltpu.HBM) if v.size > 1 else v for v in (
        signals,
        state_io,
        step_raw.T,
        row_target.reshape(-1),
        table_start,
        log_rate.reshape(1, -1),
        step_bias.reshape(1, -1),
        skip_gain.reshape(1, -1),
        norm_gain.reshape(1, -1),
    )])


def either_body(*arguments):
    one_group = (
        arguments[0].shape[0] == GROUP
        and arguments[0].shape[1] % (2 * CHUNK) == 0
        and arguments[5].shape[0] < 128
    )
    return (fused_body if one_group else body)(*arguments)


def solution(mesh):
    return jax.shard_map(
        either_body,
        mesh=mesh,
        in_specs=(
            P(("pack", "ctx"), None),
            P(("pack", "ctx"), None),
            P(("pack", "ctx"), None),
            P("pack", "ctx", None),
            P("pack", "ctx"),
            P(),
            P(),
            P(),
            P(),
        ),
        out_specs=P(("pack", "ctx"), None),
        check_vma=False,
    )
```

```python
import functools

import jax
import jax.numpy as jnp
from jax import lax
from jax.experimental import pallas as pl
from jax.experimental.pallas import tpu as pltpu
from jax.sharding import PartitionSpec as P

GROUP = 128
ROW = 8
CHUNK = 512
X_CUTS = (0.3, 0.7)
Z_CUTS = (0.6,)
GATE_PART = 1
UNROLL = 2
MESH = pl.DeviceIdType.MESH


def passed_along(block, axis, distance):
    devices = range(lax.axis_size(axis))
    route = [(i - distance, i) for i in devices if i - distance in devices]
    return lax.ppermute(block, axis, route)


def body(
    signals, state_io, step_raw, row_target, table_start, log_rate, step_bias, skip_gain, norm_gain
):
    pack_size = lax.axis_size("pack")
    ctx_size = lax.axis_size("ctx")
    row_count = row_target.shape[2]
    capacity = row_count // pack_size
    slot_count = pack_size * capacity
    inner_width = signals.shape[1] // 2
    head_count = log_rate.shape[0]
    head_width = inner_width // head_count
    state_width = state_io.shape[1] // 2
    token_count = row_count * ROW
    groups = token_count // GROUP
    targets = row_target.reshape(row_count)
    destination = targets // row_count
    row_index = jnp.arange(row_count, dtype=jnp.int32)
    earlier_rows = (destination[:, None] == destination[None, :]) & (
        row_index[None, :] < row_index[:, None]
    )
    earlier_count = jnp.sum(earlier_rows.astype(jnp.int32), axis=1)
    position = destination * capacity + earlier_count
    send_match = position[None, :] == jnp.arange(slot_count, dtype=jnp.int32)[:, None]
    send_slot = jnp.sum(jnp.where(send_match, (targets % row_count)[None, :], 0), axis=1)
    send_slot = jnp.where(jnp.any(send_match, axis=1), send_slot, -1)

    def moved(match, blocks):
        onehot = match.astype(jnp.bfloat16)
        result = jnp.einsum("sr,rtw->stw", onehot, blocks, preferred_element_type=jnp.float32)
        return result.astype(jnp.bfloat16)

    def outgoing(values):
        return moved(send_match, values.reshape(row_count, ROW, values.shape[1]))

    signal_got, io_got, raw_got, slot_got = (
        lax.all_to_all(
            outgoing(signals[:, inner_width:]), "pack", split_axis=0, concat_axis=0, tiled=True
        ),
        lax.all_to_all(outgoing(state_io), "pack", split_axis=0, concat_axis=0, tiled=True),
        lax.all_to_all(outgoing(step_raw), "pack", split_axis=0, concat_axis=0, tiled=True),
        lax.all_to_all(send_slot, "pack", split_axis=0, concat_axis=0, tiled=True),
    )
    slot_match = slot_got[None, :] == row_index[:, None]

    def arrange(values):
        return moved(slot_match, values).reshape(token_count, values.shape[-1])

    signal_in = arrange(signal_got)
    io_rows = arrange(io_got)
    raw_rows = arrange(raw_got)
    inputs = signal_in.reshape(groups, GROUP, head_count, head_width)
    b_proj = io_rows[:, :state_width].reshape(groups, GROUP, state_width)
    c_proj = io_rows[:, state_width:].reshape(groups, GROUP, state_width)
    step_size = jax.nn.softplus(raw_rows.astype(jnp.float32) + step_bias).reshape(
        groups, GROUP, head_count
    )
    log_decay = -jnp.exp(log_rate) * step_size
    causal = jnp.arange(GROUP)[:, None] >= jnp.arange(GROUP)[None, :]
    cumulative = jnp.einsum(
        "ij,kjh->kih", causal.astype(jnp.float32), log_decay, precision=lax.Precision.HIGHEST
    )
    c_dot_b = jnp.einsum("kin,kjn->kij", c_proj, b_proj, preferred_element_type=jnp.float32)
    per_head = cumulative.transpose(0, 2, 1)
    log_gaps = per_head[:, :, :, None] - per_head[:, :, None, :]
    decay_mask = jnp.exp(jnp.where(causal[None, None], log_gaps, -jnp.inf))
    scores = (c_dot_b[:, None] * decay_mask * step_size.transpose(0, 2, 1)[:, :, None, :]).astype(
        jnp.bfloat16
    )
    y_intra = jnp.einsum("khij,kjhp->kihp", scores, inputs, preferred_element_type=jnp.float32)
    to_end = jnp.exp(cumulative[:, -1:, :] - cumulative) * step_size
    weighted = (inputs.astype(jnp.float32) * to_end[..., None]).astype(jnp.bfloat16)
    local_state = jnp.einsum("kjhp,kjn->khpn", weighted, b_proj, preferred_element_type=jnp.float32)
    keep_flag = (1 - table_start.reshape(groups)).astype(jnp.float32)
    group_decay = jnp.exp(cumulative[:, -1, :])
    carry_gain = []
    carry_base = []
    gain_now = keep_flag[0] * jnp.ones((head_count,), jnp.float32)
    base_now = jnp.zeros((head_count, head_width, state_width), jnp.float32)
    for group_id in range(groups):
        if group_id > 0:
            gain_now = keep_flag[group_id] * (group_decay[group_id - 1] * gain_now)
            base_now = keep_flag[group_id] * (
                group_decay[group_id - 1][:, None, None] * base_now + local_state[group_id - 1]
            )
        carry_gain.append(gain_now)
        carry_base.append(base_now)
    leave_gain = group_decay[-1] * gain_now
    leave_base = group_decay[-1][:, None, None] * base_now + local_state[-1]
    incoming = jnp.zeros((head_count, head_width, state_width), jnp.float32)
    for hop_index in range(ctx_size - 1):
        incoming = passed_along(leave_gain[:, None, None] * incoming + leave_base, "ctx", 1)
    entering = jnp.stack(carry_gain)[:, :, None, None] * incoming[None] + jnp.stack(carry_base)
    y_state = jnp.exp(cumulative)[..., None] * jnp.einsum(
        "kin,khpn->kihp", c_proj.astype(jnp.float32), entering, precision=lax.Precision.HIGHEST
    )
    mixed = y_intra + y_state + skip_gain[None, None, :, None] * inputs.astype(jnp.float32)
    mixed = mixed.reshape(token_count, inner_width)
    gate_got = lax.all_to_all(
        outgoing(signals[:, :inner_width]), "pack", split_axis=0, concat_axis=0, tiled=True
    )
    gate_in = arrange(gate_got)
    gated = mixed * jax.nn.silu(gate_in.astype(jnp.float32))
    result = gated * lax.rsqrt(jnp.mean(gated * gated, axis=-1, keepdims=True) + 1e-05) * norm_gain
    return result.astype(jnp.bfloat16)


def exact_permute(onehot, values):
    return jnp.dot(onehot, values, preferred_element_type=jnp.float32).astype(jnp.bfloat16)


def split_sum(values):
    high = values.astype(jnp.bfloat16)
    low = (values - high.astype(jnp.float32)).astype(jnp.bfloat16)
    return jnp.concatenate([high, low], axis=1)


def fused_kernel(
    pack_size,
    ctx_size,
    head_width,
    signals_hbm,
    state_io_hbm,
    step_flip_hbm,
    row_target_hbm,
    table_start_hbm,
    log_rate_hbm,
    step_bias_hbm,
    skip_gain_hbm,
    norm_gain_hbm,
    out,
    x_in,
    z_in,
    state_io,
    step_flip,
    row_target,
    table_start,
    log_rate,
    step_bias,
    skip_gain,
    norm_gain,
    send_order,
    order,
    pieces,
    spacing,
    small,
    c_sorted,
    x_stage,
    x_got,
    z_stage,
    z_got,
    heads,
    mixed,
    squares,
    held,
    wides,
    lift,
    leave,
    enter,
    load,
    x_load,
    x_send,
    x_recv,
    z_send,
    z_recv,
    s_send,
    s_recv,
    ready,
):
    tokens = GROUP
    rows = tokens // ROW
    inner = norm_gain.shape[1]
    head_count = log_rate.shape[1]
    width = state_io.shape[1]
    state = width // 2
    block = tokens // pack_size
    chunk = CHUNK
    chunks = inner // chunk
    extra = width + 128
    x_parts = parts_of(X_CUTS, chunks)
    z_parts = parts_of(Z_CUTS, chunks)
    me = lax.axis_index("pack")
    slab = lax.axis_index("ctx")
    peers = [lax.rem(me + off, pack_size) for off in range(1, pack_size)]
    barrier = pltpu.get_barrier_semaphore()
    for peer in peers:
        pl.semaphore_signal(barrier, inc=1, device_id={"pack": peer}, device_id_type=MESH)
    for off in range(1, ctx_size):
        pl.semaphore_signal(
            barrier, inc=1, device_id={"ctx": lax.rem(slab + off, ctx_size)}, device_id_type=MESH
        )

    loads = [
        pltpu.make_async_copy(source, kept, load.at[i])
        for i, (source, kept) in enumerate(
            (
                (row_target_hbm, row_target),
                (state_io_hbm, state_io),
                (step_flip_hbm, step_flip),
                (signals_hbm.at[:, pl.ds(0, inner)], z_in),
                (table_start_hbm, table_start),
                (log_rate_hbm, log_rate),
                (step_bias_hbm, step_bias),
                (skip_gain_hbm, skip_gain),
                (norm_gain_hbm, norm_gain),
            )
        )
    ]
    x_loads = [
        pltpu.make_async_copy(
            signals_hbm.at[:, pl.ds(inner + low * chunk, (high - low) * chunk)],
            x_in.at[:, pl.ds(low * chunk, (high - low) * chunk)],
            x_load.at[k],
        )
        for k, (low, high) in enumerate(x_parts)
    ]
    for copy in loads[:3] + x_loads + loads[3:]:
        copy.start()

    lane = lax.broadcasted_iota(jnp.int32, (tokens, tokens), 1)
    sub = lax.broadcasted_iota(jnp.int32, (tokens, tokens), 0)
    head = lax.broadcasted_iota(jnp.int32, (256, chunk), 0) % 128
    column = lax.broadcasted_iota(jnp.int32, (256, chunk), 1) // head_width
    spacing[...] = head - column
    loads[0].wait()
    goal_lane = jnp.zeros((1, tokens), jnp.int32)
    goal_rows = []
    slot_rows = []
    for j in range(rows):
        target = row_target[j]
        goal = target // rows
        goal_lane = jnp.where(lane[:1] // ROW == j, goal, goal_lane)
        goal_rows.append(jnp.full((ROW, tokens), goal, jnp.int32))
        slot_rows.append(jnp.full((ROW, tokens), target - goal * rows, jnp.int32))
    goal_sub = jnp.concatenate(goal_rows, axis=0)
    slot_sub = jnp.concatenate(slot_rows, axis=0)
    earlier = (goal_sub == goal_lane) & (sub // ROW < lane // ROW) & (sub % ROW == 0)
    earlier = jnp.sum(jnp.where(earlier, 1.0, 0.0), axis=0, keepdims=True).astype(jnp.int32)
    place = (goal_lane * (rows // pack_size) + earlier) * ROW + lane[:1] % ROW
    send_order[...] = jnp.where(sub == place, 1.0, 0.0).astype(jnp.bfloat16)
    for copy in loads[1:3]:
        copy.wait()
    small[:, :width] = state_io[...]
    heads[...] = jnp.zeros(heads.shape, jnp.float32)
    heads[:head_count] = step_flip[...].astype(jnp.float32)
    spot = (slot_sub * ROW + sub % ROW).astype(jnp.float32)
    small[:, width:] = jnp.where(lane < head_count, heads[...].T, spot).astype(jnp.bfloat16)

    def x_copy(peer, slot, k):
        return pltpu.make_async_remote_copy(
            src_ref=x_stage[k].at[peer],
            dst_ref=x_got[k].at[slot],
            send_sem=x_send.at[k, peer],
            recv_sem=x_recv.at[k, slot],
            device_id={"pack": peer},
            device_id_type=MESH,
        )

    def z_copy(peer, slot, k):
        return pltpu.make_async_remote_copy(
            src_ref=z_stage[k].at[peer],
            dst_ref=z_got[k].at[slot],
            send_sem=z_send.at[k, peer],
            recv_sem=z_recv.at[k, slot],
            device_id={"pack": peer},
            device_id_type=MESH,
        )

    def s_copy(c):
        return pltpu.make_async_remote_copy(
            src_ref=leave.at[c],
            dst_ref=enter.at[c],
            send_sem=s_send.at[c],
            recv_sem=s_recv.at[c],
            device_id={"ctx": lax.rem(slab + 1, ctx_size)},
            device_id_type=MESH,
        )

    def place(c, low, first):
        return pl.multiple_of(first + (c - low) * chunk, 128)

    def stage(source, target, low, high, first):
        @pl.loop(low, high)
        def _(c):
            at = pl.multiple_of(c * chunk, chunk)
            moved = exact_permute(send_order[...], source[:, pl.ds(at, chunk)])
            target[:, :, pl.ds(place(c, low, first), chunk)] = moved.reshape(
                pack_size, block, chunk
            )

    x_stage[0][:, :, :extra] = exact_permute(send_order[...], small[...]).reshape(
        pack_size, block, extra
    )
    for k, (low, high) in enumerate(x_parts):
        x_loads[k].wait()
        stage(x_in, x_stage[k], low, high, 0 if k else extra)
        if k == 0:
            pl.semaphore_wait(barrier, pack_size + ctx_size - 2)
        for peer in peers:
            x_copy(peer, me, k).start()
    for k in range(len(x_parts)):
        x_got[k][me] = x_stage[k][me]

    for copy in loads[3:]:
        copy.wait()
    for k, (low, high) in enumerate(z_parts):
        stage(z_in, z_stage[k], low, high, 0)
        z_got[k][me] = z_stage[k][me]
    heads[0:8] = jnp.zeros((8, 128), jnp.float32)
    heads[0:1, :head_count] = log_rate[...]
    heads[1:2, :head_count] = step_bias[...]
    heads[2:3, :head_count] = skip_gain[...]

    def received_x(k):
        for peer in peers:
            x_copy(peer, peer, k).wait_recv()

    received_x(0)
    heads_got = x_got[0][:, :, width:extra].reshape(tokens, 128).astype(jnp.float32).T
    spot_lane = heads_got[head_count : head_count + 1]
    order[...] = jnp.where(spot_lane == sub.astype(jnp.float32), 1.0, 0.0).astype(jnp.bfloat16)
    maps = jnp.dot(
        order[...],
        x_got[0][:, :, :extra].reshape(tokens, extra),
        preferred_element_type=jnp.float32,
    )
    b_map = maps[:, :state]
    c_map = maps[:, state:width].astype(jnp.bfloat16)
    past = lane <= sub
    u = jnp.where(lane < head_count, maps[:, width:], 0.0) + heads[1:2, :]
    dt = jnp.maximum(u, 0.0) + jnp.log(1.0 + jnp.exp(-jnp.abs(u)))
    a = -jnp.exp(heads[0:1, :]) * dt
    cum = jnp.dot(
        jnp.where(past, 1.0, 0.0),
        a,
        preferred_element_type=jnp.float32,
        precision=lax.Precision.HIGHEST,
    )
    last = jnp.sum(a, axis=0, keepdims=True)
    mid = 0.5 * last
    dots = lax.dot_general(
        c_map,
        b_map.astype(jnp.bfloat16),
        (((1,), (1,)), ((), ())),
        preferred_element_type=jnp.float32,
    )
    c_sorted[0] = c_map
    c_sorted[1] = jnp.where(past, dots, 0.0).astype(jnp.bfloat16)
    c_sorted[2] = b_map.T.astype(jnp.bfloat16)
    keep = (1 - table_start[0, 0]).astype(jnp.float32)
    half = jnp.exp(mid)
    vectors = split_sum(
        jnp.concatenate(
            [
                half,
                keep * half,
                keep * (half * half),
                heads[2:3, :],
                jnp.zeros((4, 128), jnp.float32),
            ],
            axis=0,
        )
    )
    pieces[0:tokens] = split_sum(jnp.exp(mid - cum) * dt)
    pieces[tokens : 2 * tokens] = split_sum(jnp.exp(cum - mid))
    pieces[2 * tokens : 2 * tokens + 8] = vectors
    pieces[2 * tokens + 8 :] = jnp.zeros((8, 256), jnp.bfloat16)

    @pl.loop(0, chunks)
    def _(c):
        pick = jnp.where(spacing[...] == c * (chunk // head_width), 1.0, 0.0)
        wide = jnp.dot(
            pieces[...], pick.astype(jnp.bfloat16), preferred_element_type=jnp.float32
        )
        wides[c] = wide
        lift[c] = wide[tokens : 2 * tokens] * wide[2 * tokens + 1 : 2 * tokens + 2]

    def own_slab(c, got, low, first):
        at = pl.multiple_of(c * chunk, chunk)
        x = jnp.dot(
            order[...],
            got[:, :, pl.ds(place(c, low, first), chunk)].reshape(tokens, chunk),
            preferred_element_type=jnp.float32,
        )
        scaled = (x * wides[c, :tokens]).astype(jnp.bfloat16)
        leaving = wides[c, 2 * tokens : 2 * tokens + 1] * jnp.dot(
            c_sorted[2], scaled, preferred_element_type=jnp.float32
        )

        @pl.when(slab == 0)
        def _():
            leave[c] = leaving.astype(jnp.bfloat16)
            s_copy(c).start()

        @pl.when(slab > 0)
        def _():
            held[c] = leaving

        y = jnp.dot(c_sorted[1], scaled, preferred_element_type=jnp.float32)
        y *= wides[c, tokens : 2 * tokens]
        mixed[:, pl.ds(at, chunk)] = y + wides[c, 2 * tokens + 3 : 2 * tokens + 4] * x

    def earlier_slabs(c):
        at = pl.multiple_of(c * chunk, chunk)
        s_copy(c).wait_recv()

        @pl.when(slab < ctx_size - 1)
        def _():
            passed = wides[c, 2 * tokens + 2 : 2 * tokens + 3] * enter[c].astype(jnp.float32)
            leave[c] = (passed + held[c]).astype(jnp.bfloat16)
            s_copy(c).start()

        carried = jnp.dot(c_sorted[0], enter[c], preferred_element_type=jnp.float32)
        mixed[:, pl.ds(at, chunk)] += carried * lift[c]

    for k, (low, high) in enumerate(x_parts):
        if k > 0:
            received_x(k)
        if k == GATE_PART:
            for peer in peers:
                pl.semaphore_signal(ready, inc=1, device_id={"pack": peer}, device_id_type=MESH)
        own = functools.partial(own_slab, got=x_got[k], low=low, first=0 if k else extra)
        if k == GATE_PART:
            pl.semaphore_wait(ready, pack_size - 1)
            for part in range(len(z_parts)):
                for peer in peers:
                    z_copy(peer, me, part).start()
        pl.loop(low, high, unroll=UNROLL)(own)
        if k > 0:

            @pl.when(slab > 0)
            def _():
                pl.loop(*x_parts[k - 1], unroll=UNROLL)(earlier_slabs)

    late = x_parts[-1][0]

    @pl.when((slab > 0) & (slab < ctx_size - 1))
    def _():
        pl.loop(late, chunks, unroll=UNROLL)(earlier_slabs)

    squares[...] = jnp.zeros(squares.shape, jnp.float32)
    for peer in peers:
        for k in range(len(x_parts)):
            x_copy(peer, me, k).wait_send()

    @pl.when(slab < ctx_size - 1)
    def _():
        @pl.loop(0, chunks)
        def _(c):
            s_copy(c).wait_send()


    def gate(c, got, low):
        at = pl.multiple_of(c * chunk, chunk)
        z = jnp.dot(
            order[...],
            got[:, :, pl.ds(place(c, low, 0), chunk)].reshape(tokens, chunk),
            preferred_element_type=jnp.float32,
        )
        half_z = 0.5 * z
        g = mixed[:, pl.ds(at, chunk)] * (half_z * jnp.tanh(half_z) + half_z)
        mixed[:, pl.ds(at, chunk)] = g
        g = g * g
        total = g[:, :128]
        for k in range(1, chunk // 128):
            total += g[:, k * 128 : (k + 1) * 128]
        squares[...] += total

    for k, (low, high) in enumerate(z_parts):
        for peer in peers:
            z_copy(peer, peer, k).wait_recv()
        gate_part = functools.partial(gate, got=z_got[k], low=low)
        if low < late:
            pl.loop(low, min(late, high), unroll=UNROLL)(gate_part)
        if high > late:

            @pl.when(slab < ctx_size - 1)
            def _():
                pl.loop(max(low, late), high, unroll=UNROLL)(gate_part)

            @pl.when(slab == ctx_size - 1)
            def _():
                @pl.loop(max(low, late), high)
                def _(c):
                    earlier_slabs(c)
                    gate_part(c)

        if k < len(z_parts) - 1:
            for peer in peers:
                z_copy(peer, me, k).wait_send()

    mean = jnp.sum(squares[...], axis=1, keepdims=True) * (1.0 / inner)
    squares[...] = jnp.broadcast_to(lax.rsqrt(mean + 1e-05), squares.shape)

    @pl.loop(0, chunks, unroll=2)
    def _(c):
        at = pl.multiple_of(c * chunk, chunk)
        scale = jnp.concatenate([squares[...]] * (chunk // 128), axis=1)
        normed = mixed[:, pl.ds(at, chunk)] * scale * norm_gain[:, pl.ds(at, chunk)]
        out[:, pl.ds(at, chunk)] = normed.astype(jnp.bfloat16)

    for peer in peers:
        z_copy(peer, me, len(z_parts) - 1).wait_send()


def parts_of(cuts, chunks):
    ends = [max(1, round(cut * chunks)) for cut in cuts] + [chunks]
    return list(zip([0] + ends[:-1], ends))


def fused_body(
    signals, state_io, step_raw, row_target, table_start, log_rate, step_bias, skip_gain, norm_gain
):
    pack_size = lax.axis_size("pack")
    ctx_size = lax.axis_size("ctx")
    tokens = signals.shape[0]
    inner = signals.shape[1] // 2
    width = state_io.shape[1]
    state = width // 2
    head_count = log_rate.shape[0]
    block = tokens // pack_size
    chunks = inner // CHUNK
    extra = width + 128
    x_count = len(X_CUTS) + 1
    z_count = len(Z_CUTS) + 1
    hbm = pl.BlockSpec(memory_space=pltpu.HBM)
    x_buffers = [
        pltpu.VMEM((pack_size, block, (high - low) * CHUNK + (0 if k else extra)), jnp.bfloat16)
        for k, (low, high) in enumerate(parts_of(X_CUTS, chunks))
    ]
    z_buffers = [
        pltpu.VMEM((pack_size, block, (high - low) * CHUNK), jnp.bfloat16)
        for low, high in parts_of(Z_CUTS, chunks)
    ]
    return pl.pallas_call(
        functools.partial(fused_kernel, pack_size, ctx_size, inner // head_count),
        out_shape=jax.ShapeDtypeStruct((tokens, inner), jnp.bfloat16),
        in_specs=[hbm] * 9,
        out_specs=pl.BlockSpec(memory_space=pltpu.VMEM),
        scratch_shapes=[
            pltpu.VMEM((tokens, inner), jnp.bfloat16),
            pltpu.VMEM((tokens, inner), jnp.bfloat16),
            pltpu.VMEM((tokens, width), jnp.bfloat16),
            pltpu.VMEM((head_count, tokens), jnp.bfloat16),
            pltpu.SMEM((tokens // ROW,), jnp.int32),
            pltpu.SMEM((1, 1), jnp.int32),
            pltpu.VMEM((1, head_count), jnp.float32),
            pltpu.VMEM((1, head_count), jnp.float32),
            pltpu.VMEM((1, head_count), jnp.float32),
            pltpu.VMEM((1, inner), jnp.float32),
            pltpu.VMEM((tokens, tokens), jnp.bfloat16),
            pltpu.VMEM((tokens, tokens), jnp.bfloat16),
            pltpu.VMEM((2 * tokens + 16, 256), jnp.bfloat16),
            pltpu.VMEM((256, CHUNK), jnp.int32),
            pltpu.VMEM((tokens, extra), jnp.bfloat16),
            pltpu.VMEM((3, tokens, state), jnp.bfloat16),
            x_buffers,
            x_buffers,
            z_buffers,
            z_buffers,
            pltpu.VMEM((128, tokens), jnp.float32),
            pltpu.VMEM((tokens, inner), jnp.float32),
            pltpu.VMEM((tokens, 128), jnp.float32),
            pltpu.VMEM((chunks, state, CHUNK), jnp.float32),
            pltpu.VMEM((chunks, 2 * tokens + 16, CHUNK), jnp.float32),
            pltpu.VMEM((chunks, tokens, CHUNK), jnp.float32),
            pltpu.VMEM((chunks, state, CHUNK), jnp.bfloat16),
            pltpu.VMEM((chunks, state, CHUNK), jnp.bfloat16),
            pltpu.SemaphoreType.DMA((9,)),
            pltpu.SemaphoreType.DMA((x_count,)),
            pltpu.SemaphoreType.DMA((x_count, pack_size)),
            pltpu.SemaphoreType.DMA((x_count, pack_size)),
            pltpu.SemaphoreType.DMA((z_count, pack_size)),
            pltpu.SemaphoreType.DMA((z_count, pack_size)),
            pltpu.SemaphoreType.DMA((chunks,)),
            pltpu.SemaphoreType.DMA((chunks,)),
            pltpu.SemaphoreType.REGULAR,
        ],
        compiler_params=pltpu.CompilerParams(
            collective_id=0, has_side_effects=True, vmem_limit_bytes=32 * 1024 * 1024
        ),
    )(*[pltpu.with_memory_space_constraint(v, pltpu.HBM) if v.size > 1 else v for v in (
        signals,
        state_io,
        step_raw.T,
        row_target.reshape(-1),
        table_start,
        log_rate.reshape(1, -1),
        step_bias.reshape(1, -1),
        skip_gain.reshape(1, -1),
        norm_gain.reshape(1, -1),
    )])


def either_body(*arguments):
    one_group = (
        arguments[0].shape[0] == GROUP
        and arguments[0].shape[1] % (2 * CHUNK) == 0
        and arguments[5].shape[0] < 128
    )
    return (fused_body if one_group else body)(*arguments)


def solution(mesh):
    return jax.shard_map(
        either_body,
        mesh=mesh,
        in_specs=(
            P(("pack", "ctx"), None),
            P(("pack", "ctx"), None),
            P(("pack", "ctx"), None),
            P("pack", "ctx", None),
            P("pack", "ctx"),
            P(),
            P(),
            P(),
            P(),
        ),
        out_specs=P(("pack", "ctx"), None),
        check_vma=False,
    )
```
